256 devices in a mesh: section: 32 (over y, x, z_lo), dp: 8 (over z_hi, core).
Axes of the slice: x: 4, y: 4, z: 8 (z_hi: 4, z_lo: 2; z = z_hi * 2 + z_lo), core: 2. Of those that a mesh axis runs over, the one named last changes fastest.
Arguments:
- act_down: bfloat16 [32, 2, 2048, 1024], P('section', None, 'dp'), may hold values from -6 to 6
- act_up: bfloat16 [32, 2, 2048, 1024], P('section', None, 'dp'), may hold values from -6 to 6
- grad_down: bfloat16 [32, 2048, 1024], P('section', 'dp'), may hold values from -1.5 to 1.5
- grad_up: bfloat16 [32, 2048, 1024], P('section', 'dp'), may hold values from -1.5 to 1.5
- seed_down: bfloat16 [2048, 1024], P('dp'), may hold values from -1.5 to 1.5
- seed_up: bfloat16 [2048, 1024], P('dp'), may hold values from -1.5 to 1.5
- gain_down: float32 [32, 1024], P('section'), as said below
- qkv_down: bfloat16 [32, 1024, 768], P('section'), as said below
- outproj_down: bfloat16 [32, 512, 1024], P('section'), as said below
- gain_up: float32 [32, 1024], P('section'), as said below
- qkv_up: bfloat16 [32, 1024, 768], P('section'), as said below
- outproj_up: bfloat16 [32, 512, 1024], P('section'), as said below
- doc_offsets: int32 [2, 32, 2, 8], P(None, 'section', None, 'dp'), may hold values from 1 to 255
- slot_order: int32 [2, 32, 2], P(None, 'section'), may hold values from 0 to 1, each once within a row
Outputs:
- input_grads: bfloat16 [2, 32, 2, 2048, 1024], P(None, 'section', None, 'dp')
- grad_gain: float32 [32, 1024], P('section', 'dp')
- grad_qkv: float32 [32, 1024, 768], P('section', 'dp')
- grad_outproj: float32 [32, 512, 1024], P('section', 'dp')
The draws below stay inside these ranges and needn't reach their ends.
Inputs may be any that keep to these rules, and one draw needn't show every extreme that they name: `gain_down`: the down copy of every layer. `qkv_down`: the down copy of every layer. `outproj_down`: the down copy of every layer. gain_up[s] equals gain_down[31 - s]. qkv_up[s] equals qkv_down[31 - s]. outproj_up[s] equals outproj_down[31 - s]. `doc_offsets`: each sequence holds two documents; the value is the position where the second begins. `slot_order`: each row of a direction and section names 0 and 1 once each.
All inputs are finite; a program needn't handle non-finite values.
Results may differ from the reference program's by a relative error of at most 0.015.
Values may be sent and summed in bfloat16 or wider, within the bound.
A program may use at most 128 MiB of HBM per device.

```python
import math
import jax
import jax.numpy as jnp
from jax import lax

D = 1024
HEADS = 8
KV_HEADS = 2
SEQ = 256
QW = 512
QKV = 768
LAYERS = 32
REPLICAS = 8
TOKENS = 2048


def mirrored_layers(key):
    base = jax.random.fold_in(key, 31)
    key_gain = jax.random.fold_in(base, 1)
    key_qkv = jax.random.fold_in(base, 2)
    key_out = jax.random.fold_in(base, 3)
    gains = jax.random.uniform(key_gain, (LAYERS, D), jnp.float32, 0.6, 1.4)
    qkv = jax.random.normal(key_qkv, (LAYERS, D, QKV), jnp.float32) / math.sqrt(D)
    outproj = jax.random.normal(key_out, (LAYERS, QW, D), jnp.float32) / math.sqrt(QW)
    return (gains, qkv.astype(jnp.bfloat16), outproj.astype(jnp.bfloat16))


def draw_gain_down(key, part):
    return mirrored_layers(key)[0]


def draw_qkv_down(key, part):
    return mirrored_layers(key)[1]


def draw_outproj_down(key, part):
    return mirrored_layers(key)[2]


def draw_gain_up(key, part):
    return jnp.flip(mirrored_layers(key)[0], axis=0)


def draw_qkv_up(key, part):
    return jnp.flip(mirrored_layers(key)[1], axis=0)


def draw_outproj_up(key, part):
    return jnp.flip(mirrored_layers(key)[2], axis=0)


def place_ends(drawn, key, smallest, top_value):
    longest = drawn.shape.index(max(drawn.shape))
    spots = []
    for shift in (0, 1):
        where = [jax.random.randint(jax.random.fold_in(key, axis), (), 0, length) for axis, length in enumerate(drawn.shape)]
        where[longest] = (where[longest] + shift) % drawn.shape[longest]
        spots.append(tuple(where))
    return drawn.at[spots[0]].set(smallest).at[spots[1]].set(top_value)


def block_levels(rng, shape, shards, low, top_value):
    gain, own = 1.0, jax.random.fold_in(rng, 6)
    for dim, shards_of in shards:
        steps = jnp.exp(jax.random.uniform(jax.random.fold_in(own, dim), (shards_of,), jnp.float32, low / len(shards), top_value / len(shards)))
        gain = gain * jnp.repeat(steps, shape[dim] // shards_of).reshape([-1 if axis == dim else 1 for axis in range(len(shape))])
    return gain


def centred(own_key, shape, spread, limit, shards=(), kind=jnp.bfloat16):
    factor_of = block_levels(own_key, shape, shards, -0.22, 0.18) if shards else 1.0
    result = jax.random.normal(own_key, shape, jnp.float32) * spread * factor_of
    return jnp.minimum(jnp.maximum(result, -limit), limit).astype(kind)


def setup_inputs(seed: int = 0) -> dict:
    streams_of = jax.random.split(jax.random.key(seed), 15)
    return {
        "act_down": centred(streams_of[0], (LAYERS, 2, TOKENS, D), 1.0, 6.0, ((0, 32), (2, 8))),
        "act_up": centred(streams_of[1], (LAYERS, 2, TOKENS, D), 1.0, 6.0, ((0, 32), (2, 8))),
        "grad_down": centred(streams_of[2], (LAYERS, TOKENS, D), 0.25, 1.5, ((0, 32), (1, 8))),
        "grad_up": centred(streams_of[3], (LAYERS, TOKENS, D), 0.25, 1.5, ((0, 32), (1, 8))),
        "seed_down": centred(streams_of[4], (TOKENS, D), 0.25, 1.5, ((0, 8),)),
        "seed_up": centred(streams_of[5], (TOKENS, D), 0.25, 1.5, ((0, 8),)),
        "gain_down": draw_gain_down(jax.random.fold_in(streams_of[14], 71), 0),
        "qkv_down": draw_qkv_down(jax.random.fold_in(streams_of[14], 71), 0),
        "outproj_down": draw_outproj_down(jax.random.fold_in(streams_of[14], 71), 0),
        "gain_up": draw_gain_up(jax.random.fold_in(streams_of[14], 71), 0),
        "qkv_up": draw_qkv_up(jax.random.fold_in(streams_of[14], 71), 0),
        "outproj_up": draw_outproj_up(jax.random.fold_in(streams_of[14], 71), 0),
        "doc_offsets": place_ends(jax.random.randint(streams_of[12], (2, LAYERS, 2, REPLICAS), 1, SEQ), jax.random.fold_in(streams_of[12], 1), 1, SEQ - 1).astype(jnp.int32),
        "slot_order": jax.vmap(lambda own: jax.random.permutation(own, 2))(jax.random.split(streams_of[13], 2 * LAYERS)).reshape((2, LAYERS, 2)).astype(jnp.int32),
    }


EPSILON = 1e-05

def backward_layer(inputs, gain_vec, qkv_weight, out_weight, offset, upstream):
    seq_len = inputs.shape[0]
    query_width = out_weight.shape[0]
    pair_width = (qkv_weight.shape[1] - query_width) // 2
    group_size = HEADS // KV_HEADS
    head_width = query_width // HEADS
    score_scale = head_width ** (-0.5)
    xfloat = inputs.astype(jnp.float32)
    inverse = lax.rsqrt(lax.optimization_barrier(jnp.mean(xfloat * xfloat, axis=1, keepdims=True)) + EPSILON)
    scaled = xfloat * inverse
    normed = (scaled * gain_vec).astype(jnp.bfloat16)
    project = jnp.dot(normed, qkv_weight, preferred_element_type=jnp.float32).astype(jnp.bfloat16)
    queries = project[:, :query_width].reshape(seq_len, KV_HEADS, group_size, head_width).astype(jnp.float32)
    keys_all = project[:, query_width:query_width + pair_width].reshape(seq_len, KV_HEADS, head_width).astype(jnp.float32)
    values = project[:, query_width + pair_width:].reshape(seq_len, KV_HEADS, head_width).astype(jnp.float32)
    positions = jnp.arange(seq_len, dtype=jnp.int32)
    second_doc = positions >= offset
    allowed = (positions[None, :] <= positions[:, None]) & (second_doc[None, :] == second_doc[:, None])
    scores = jnp.einsum('igha,jga->ghij', queries, keys_all) * score_scale
    scores = jnp.where(allowed, scores, -1e+30)
    row_top = lax.optimization_barrier(jnp.max(scores, axis=3, keepdims=True))
    raised = jnp.exp(scores - row_top)
    soft_weights = raised / lax.optimization_barrier(jnp.sum(raised, axis=3, keepdims=True))
    soft_low = soft_weights.astype(jnp.bfloat16)
    soft_wide = soft_low.astype(jnp.float32)
    attended = jnp.einsum('ghij,jga->igha', soft_wide, values).reshape(seq_len, query_width).astype(jnp.bfloat16)
    grad_out = jnp.dot(attended.T, upstream, preferred_element_type=jnp.float32)
    grad_attended = jnp.dot(upstream, out_weight.T, preferred_element_type=jnp.float32).astype(jnp.bfloat16)
    grad_heads = grad_attended.reshape(seq_len, KV_HEADS, group_size, head_width).astype(jnp.float32)
    grad_values = jnp.einsum('ghij,igha->jga', soft_wide, grad_heads)
    grad_soft = jnp.einsum('igha,jga->ghij', grad_heads, values)
    grad_scores = (soft_weights * (grad_soft - lax.optimization_barrier(jnp.sum(soft_weights * grad_soft, axis=3, keepdims=True))) * score_scale).astype(jnp.bfloat16)
    scores_wide = grad_scores.astype(jnp.float32)
    grad_queries = jnp.einsum('ghij,jga->igha', scores_wide, keys_all)
    grad_keys = jnp.einsum('ghij,igha->jga', scores_wide, queries)
    grad_project = jnp.concatenate([grad_queries.reshape(seq_len, query_width), grad_keys.reshape(seq_len, pair_width), grad_values.reshape(seq_len, pair_width)], axis=1).astype(jnp.bfloat16)
    grad_qkv = jnp.dot(normed.T, grad_project, preferred_element_type=jnp.float32)
    grad_normed = jnp.dot(grad_project, qkv_weight.T, preferred_element_type=jnp.float32)
    grad_gain = lax.optimization_barrier(jnp.sum(grad_normed * scaled, axis=0))
    grad_hat = grad_normed * gain_vec
    grad_inputs = upstream.astype(jnp.float32) + inverse * (grad_hat - scaled * lax.optimization_barrier(jnp.mean(grad_hat * scaled, axis=1, keepdims=True)))
    return (grad_inputs.astype(jnp.bfloat16), grad_gain, grad_qkv, grad_out)

def rounded_sum(term):
    low = lax.optimization_barrier(term.astype(jnp.bfloat16))
    return lax.optimization_barrier(jnp.sum(low.astype(jnp.float32), axis=0))

def run_direction(acts, first_grads, seeds, gains, qkv_weights, out_weights, offsets, order_rows, from_top):
    first_zero = order_rows[:, 0] == 0
    second_zero = order_rows[:, 1] == 0
    acts_one = jnp.where(first_zero[:, None, None], acts[:, 0], acts[:, 1]).reshape(LAYERS, REPLICAS, SEQ, D)
    acts_two = jnp.where(second_zero[:, None, None], acts[:, 0], acts[:, 1]).reshape(LAYERS, REPLICAS, SEQ, D)
    offs_one = jnp.where(first_zero[:, None], offsets[:, 0], offsets[:, 1])
    offs_two = jnp.where(second_zero[:, None], offsets[:, 0], offsets[:, 1])
    upstream_one = first_grads.reshape(LAYERS, REPLICAS, SEQ, D)
    batched = jax.vmap(backward_layer, in_axes=(0, None, None, None, 0, 0))

    def section_step(carry, items):
        acts_a, acts_b, upstream_a, gain_vec, qkv_weight, out_weight, offs_a, offs_b = items
        one = batched(acts_a, gain_vec, qkv_weight, out_weight, offs_a, upstream_a)
        two = batched(acts_b, gain_vec, qkv_weight, out_weight, offs_b, carry)
        gain_sum = rounded_sum(one[1] + two[1])
        qkv_sum = rounded_sum(one[2] + two[2])
        out_sum = rounded_sum(one[3] + two[3])
        return (one[0], (one[0], two[0], gain_sum, qkv_sum, out_sum))
    items = (acts_one, acts_two, upstream_one, gains, qkv_weights, out_weights, offs_one, offs_two)
    seeds_split = seeds.reshape(REPLICAS, SEQ, D)
    unused, stacked = lax.scan(section_step, seeds_split, items, reverse=from_top)
    grads_one, grads_two, gain_sums, qkv_sums, out_sums = stacked
    input_grads = jnp.stack([grads_one, grads_two], axis=1).reshape(LAYERS, 2, TOKENS, D)
    return (input_grads, gain_sums, qkv_sums, out_sums)

def reference(act_down, act_up, grad_down, grad_up, seed_down, seed_up, gain_down, qkv_down, outproj_down, gain_up, qkv_up, outproj_up, doc_offsets, slot_order):
    down = run_direction(act_down, grad_down, seed_down, gain_down, qkv_down, outproj_down, doc_offsets[0], slot_order[0], True)
    upper = run_direction(act_up, grad_up, seed_up, gain_up, qkv_up, outproj_up, doc_offsets[1], slot_order[1], False)
    input_grads = jnp.stack([down[0], upper[0]], axis=0)
    grad_gain = down[1] + jnp.flip(upper[1], axis=0)
    grad_qkv = down[2] + jnp.flip(upper[2], axis=0)
    grad_outproj = down[3] + jnp.flip(upper[3], axis=0)
    return (input_grads, grad_gain, grad_qkv, grad_outproj)
```

```python
import jax
import jax.numpy as jnp
from jax import lax
from jax.experimental import pallas as pl
from jax.experimental.pallas import tpu as pltpu
from jax.sharding import PartitionSpec as P

F32, BF16 = jnp.float32, jnp.bfloat16
EPSILON = 1e-05
D, SEQ, HEADS, GROUP, HD = 1024, 256, 8, 4, 64
QW, QKV = 512, 768
ROWS = 32
PIECE = QKV + QW + 16


def nn(a, b):
    return jnp.dot(a, b, preferred_element_type=F32)


def nt(a, b):
    return lax.dot_general(a, b, (((1,), (1,)), ((), ())), preferred_element_type=F32)


def norm_rows(x, gain, normed, inverse):
    @pl.loop(0, SEQ // ROWS)
    def _(step):
        rows = pl.ds(pl.multiple_of(step * ROWS, ROWS), ROWS)
        xf = x[rows, :].astype(F32)
        inv = lax.rsqrt(jnp.mean(xf * xf, axis=1, keepdims=True) + EPSILON)
        normed[rows, :] = (xf * inv * gain[...]).astype(BF16)
        inverse[rows, :] = jnp.broadcast_to(inv, (ROWS, 128))


def forward(offset, normed, qkv, keep):
    proj_t, keys, values, soft, soft_low, att_t = keep
    for n in range(3):
        cols = slice(n * 256, n * 256 + 256)
        part = nn(normed[...], qkv[:, cols])
        proj_t[cols, :] = part.T.astype(BF16)
        if n == 2:
            low = part.astype(BF16)
            keys[0], keys[1] = low[:, :64], low[:, 64:128]
            values[0], values[1] = low[:, 128:192], low[:, 192:256]

    @pl.loop(0, HEADS)
    def _(head):
        group = head // GROUP
        rows = pl.ds(pl.multiple_of(head * HD, HD), HD)
        scores = nn(keys[group], proj_t[rows, :])
        for half, depth in ((0, 128), (1, 256)):
            cols = slice(half * 128, half * 128 + 128)
            at_key = lax.broadcasted_iota(jnp.int32, (depth, 128), 0)
            at_query = lax.broadcasted_iota(jnp.int32, (depth, 128), 1) + half * 128
            allowed = (at_key <= at_query) & ((at_query < offset) | (at_key >= offset))
            part = jnp.where(allowed, scores[:depth, cols] * (HD**-0.5), -1e30)
            raised = jnp.exp(part - jnp.max(part, axis=0, keepdims=True))
            weights = raised * (1.0 / jnp.sum(raised, axis=0, keepdims=True))
            soft[head, :depth, cols] = weights
            soft_low[head, :depth, cols] = weights.astype(BF16)
        soft_low[head, 128:, :128] = jnp.zeros((128, 128), BF16)
        value_rows = pl.ds(pl.multiple_of(QW + 128 + group * HD, HD), HD)
        att_t[rows, :] = nn(proj_t[value_rows, :], soft_low[head]).astype(BF16)


def backward(x, gain, inverse, qkv, outproj, upstream, keep, work, grad_t, gain_sum, result):
    proj_t, keys, values, soft, soft_low, att_t = keep
    att_grad, score_grad, key_sum, value_sum, grad, normed_grad = work
    for m in range(2):
        rows = slice(m * 256, m * 256 + 256)
        att_grad[rows, :] = nt(outproj[rows, :], upstream[...]).astype(BF16)
    key_sum[...] = jnp.zeros_like(key_sum)
    value_sum[...] = jnp.zeros_like(value_sum)
    score_grad[128:, :128] = jnp.zeros((128, 128), BF16)

    @pl.loop(0, HEADS)
    def _(head):
        group = head // GROUP
        rows = pl.ds(pl.multiple_of(head * HD, HD), HD)
        low = att_grad[rows, :]
        soft_grad = nn(values[group], low)
        for half, depth in ((0, 128), (1, 256)):
            cols = slice(half * 128, half * 128 + 128)
            weights = soft[head, :depth, cols]
            part = soft_grad[:depth, cols]
            total = jnp.sum(weights * part, axis=0, keepdims=True)
            score_grad[:depth, cols] = (weights * (part - total) * (HD**-0.5)).astype(BF16)
        key_rows = pl.ds(pl.multiple_of(QW + group * HD, HD), HD)
        grad_t[rows, :] = nn(proj_t[key_rows, :], score_grad[...]).astype(BF16)
        key_sum[group] += nt(proj_t[rows, :], score_grad[...])
        value_sum[group] += nt(low, soft_low[head])

    for g in range(2):
        grad_t[QW + g * HD : QW + g * HD + HD, :] = key_sum[g].astype(BF16)
        grad_t[QW + 128 + g * HD : QW + 128 + g * HD + HD, :] = value_sum[g].astype(BF16)
    for n in range(3):
        cols = slice(n * 256, n * 256 + 256)
        grad[:, cols] = grad_t[cols, :].T
    for n in range(4):
        cols = slice(n * 256, n * 256 + 256)
        normed_grad[:, cols] = nt(grad[...], qkv[cols, :])

    @pl.loop(0, SEQ // ROWS)
    def _(step):
        rows = pl.ds(pl.multiple_of(step * ROWS, ROWS), ROWS)
        inv = inverse[rows, :][:, :1]
        scaled = x[rows, :].astype(F32) * inv
        hat = normed_grad[rows, :]
        both = hat * scaled
        partial = both[:8]
        for k in range(1, ROWS // 8):
            partial = partial + both[k * 8 : k * 8 + 8]
        gain_sum[...] += partial
        mean = jnp.mean(both * gain[...], axis=1, keepdims=True)
        moved = inv * (hat * gain[...] - scaled * mean)
        result[rows, :] = (upstream[rows, :].astype(F32) + moved).astype(BF16)


def weight_terms(q, grad_t, normed, att_t, upstream, gain_sum, piece):
    cols = pl.ds(pl.multiple_of(q * 256, 256), 256)
    for m in range(3):
        rows = slice(m * 256, m * 256 + 256)
        part = nn(grad_t[0][rows, :], normed[0][:, cols]) + nn(grad_t[1][rows, :], normed[1][:, cols])
        for core in range(2):
            piece[core, rows, :] = part[:, core * 128 : core * 128 + 128].astype(BF16)
    heads = pl.ds(pl.multiple_of(q * 128, 128), 128)
    for n in range(4):
        wide = slice(n * 256, n * 256 + 256)
        part = nn(att_t[0][heads, :], upstream[0][:, wide]) + nn(att_t[1][heads, :], upstream[1][:, wide])
        for core in range(2):
            for k in range(2):
                at = QKV + (2 * n + k) * HD
                block = part[core * HD : core * HD + HD, k * 128 : k * 128 + 128]
                piece[core, at : at + HD, :] = block.astype(BF16)
    for core in range(2):
        lanes = pl.ds(pl.multiple_of(q * 256 + core * 128, 128), 128)
        row = jnp.sum(gain_sum[:, lanes], axis=0, keepdims=True)
        piece[core, QKV + QW :, :] = jnp.broadcast_to(row, (16, 128)).astype(BF16)


KEEP = [
    pltpu.VMEM((QKV, SEQ), BF16),
    pltpu.VMEM((2, SEQ, HD), BF16),
    pltpu.VMEM((2, SEQ, HD), BF16),
    pltpu.VMEM((HEADS, SEQ, SEQ), F32),
    pltpu.VMEM((HEADS, SEQ, SEQ), BF16),
]
WORK = [
    pltpu.VMEM((QW, SEQ), BF16),
    pltpu.VMEM((SEQ, SEQ), BF16),
    pltpu.VMEM((2, HD, SEQ), F32),
    pltpu.VMEM((2, HD, SEQ), F32),
    pltpu.VMEM((SEQ, QKV), BF16),
    pltpu.VMEM((SEQ, D), F32),
]
INV = pltpu.VMEM((SEQ, 128), F32)


def first_kernel(picks, x, gain, qkv, outproj, upstream, result, normed, grad_t, att_t, gain_sum, inverse, *scratch):
    keep, work = (*scratch[:5], att_t), scratch[5:]
    gain_sum[...] = jnp.zeros_like(gain_sum)
    norm_rows(x, gain, normed, inverse)
    forward(picks[1], normed, qkv, keep)
    backward(x, gain, inverse, qkv, outproj, upstream, keep, work, grad_t, gain_sum, result)


def second_kernel(
    picks, x, gain, qkv, outproj, upstream, upstream_one, normed_one, grad_one, att_one, gain_one,
    result, pieces, inverse, normed, grad_t, att_t, gain_sum, *scratch,
):
    keep, work = (*scratch[:5], att_t), scratch[5:]
    gain_sum[...] = gain_one[...]
    norm_rows(x, gain, normed, inverse)
    forward(picks[1], normed, qkv, keep)
    backward(x, gain, inverse, qkv, outproj, upstream, keep, work, grad_t, gain_sum, result)

    @pl.loop(0, 4)
    def _(q):
        weight_terms(
            q, (grad_one, grad_t), (normed_one, normed), (att_one, att_t),
            (upstream_one, upstream), gain_sum, pieces.at[q],
        )


def full(shape):
    return pl.BlockSpec(shape, lambda i, picks: (0,) * len(shape), pipeline_mode=pl.Buffered(1))


def chosen():
    return pl.BlockSpec((None, SEQ, D), lambda i, picks: (picks[0], 0, 0), pipeline_mode=pl.Buffered(1))


PARAMS = pltpu.CompilerParams(vmem_limit_bytes=48 * 2**20)
WEIGHTS = ((1, D), (D, QKV), (QW, D), (SEQ, D))
KEPT = ((SEQ, D), (QKV, SEQ), (QW, SEQ), (8, D))
KEPT_TYPES = (BF16, BF16, BF16, F32)


def slot_one(picks, acts, gain, qkv, outproj, upstream):
    return pl.pallas_call(
        first_kernel,
        grid_spec=pltpu.PrefetchScalarGridSpec(
            num_scalar_prefetch=1,
            grid=(1,),
            in_specs=[chosen(), *(full(s) for s in WEIGHTS)],
            out_specs=[full((SEQ, D)), *(full(s) for s in KEPT)],
            scratch_shapes=[INV, *KEEP, *WORK],
        ),
        out_shape=[
            jax.ShapeDtypeStruct((SEQ, D), BF16),
            *(jax.ShapeDtypeStruct(s, t) for s, t in zip(KEPT, KEPT_TYPES)),
        ],
        cost_estimate=pl.CostEstimate(flops=2 * 10**9, bytes_accessed=6 * 10**6, transcendentals=5 * 10**5),
        compiler_params=PARAMS,
    )(picks, acts, gain, qkv, outproj, upstream)


def slot_two(picks, acts, gain, qkv, outproj, upstream, upstream_one, kept):
    return pl.pallas_call(
        second_kernel,
        grid_spec=pltpu.PrefetchScalarGridSpec(
            num_scalar_prefetch=1,
            grid=(1,),
            in_specs=[chosen(), *(full(s) for s in WEIGHTS), full((SEQ, D)), *(full(s) for s in KEPT)],
            out_specs=[full((SEQ, D)), full((4, 2, PIECE, 128))],
            scratch_shapes=[
                INV,
                *(pltpu.VMEM(s, t) for s, t in zip(KEPT, KEPT_TYPES)),
                *KEEP,
                *WORK,
            ],
        ),
        out_shape=[
            jax.ShapeDtypeStruct((SEQ, D), BF16),
            jax.ShapeDtypeStruct((4, 2, PIECE, 128), BF16),
        ],
        cost_estimate=pl.CostEstimate(flops=3 * 10**9, bytes_accessed=10 * 10**6, transcendentals=5 * 10**5),
        compiler_params=PARAMS,
    )(picks, acts, gain, qkv, outproj, upstream, upstream_one, *kept)


def shards(
    act_down, act_up, grad_down, grad_up, seed_down, seed_up, gain_down, qkv_down, outproj_down,
    gain_up, qkv_up, outproj_up, doc_offsets, slot_order,
):
    count = lax.axis_size("section")
    section = lax.axis_index("section")
    order = slot_order[:, 0]
    offsets = jnp.take_along_axis(doc_offsets[:, 0, :, 0], order, axis=1)
    picks = jnp.stack([order, offsets], axis=2)
    up = (act_up[0], gain_up, qkv_up[0], outproj_up[0])
    down = (act_down[0], gain_down, qkv_down[0], outproj_down[0])
    up_one, *up_kept = slot_one(picks[1, 0], *up, grad_up[0])
    from_below = lax.ppermute(up_one, "section", [(s, s + 1) for s in range(count - 1)])
    down_one, *down_kept = slot_one(picks[0, 0], *down, grad_down[0])
    from_above = lax.ppermute(down_one, "section", [(s, s - 1) for s in range(1, count)])
    up_stream = jnp.where(section == 0, seed_up, from_below)
    down_stream = jnp.where(section == count - 1, seed_down, from_above)
    up_two, up_pieces = slot_two(picks[1, 1], *up, up_stream, grad_up[0], up_kept)
    up_sum = lax.psum_scatter(up_pieces.reshape(8, PIECE, 128), "dp", scatter_dimension=0, tiled=True)
    down_two, down_pieces = slot_two(picks[0, 1], *down, down_stream, grad_down[0], down_kept)
    down_sum = lax.psum_scatter(down_pieces.reshape(8, PIECE, 128), "dp", scatter_dimension=0, tiled=True)
    mirror = lax.ppermute(up_sum, "section", [(s, count - 1 - s) for s in range(count)])
    total = down_sum[0].astype(F32) + mirror[0].astype(F32)
    grad_qkv = total[:QKV].T
    grad_out = total[QKV : QKV + QW].reshape(8, HD, 128).transpose(1, 0, 2).reshape(HD, D)
    grad_gain = total[QKV + QW]
    input_grads = jnp.stack([jnp.stack([down_one, down_two]), jnp.stack([up_one, up_two])])[:, None]
    return input_grads, grad_gain[None], grad_qkv[None], grad_out[None]


def solution(mesh):
    return jax.shard_map(
        shards,
        mesh=mesh,
        in_specs=(
            P("section", None, "dp", None),
            P("section", None, "dp", None),
            P("section", "dp", None),
            P("section", "dp", None),
            P("dp", None),
            P("dp", None),
            P("section", None),
            P("section", None, None),
            P("section", None, None),
            P("section", None),
            P("section", None, None),
            P("section", None, None),
            P(None, "section", None, "dp"),
            P(None, "section", None),
        ),
        out_specs=(
            P(None, "section", None, "dp", None),
            P("section", "dp"),
            P("section", "dp", None),
            P("section", "dp", None),
        ),
        check_vma=False,
    )
```

```python
import functools

import jax
import jax.numpy as jnp
from jax import lax
from jax.experimental import pallas as pl
from jax.experimental.pallas import tpu as pltpu
from jax.sharding import PartitionSpec as P

F32, BF16 = jnp.float32, jnp.bfloat16
EPSILON = 1e-05
D, SEQ, HEADS, GROUP, HD = 1024, 256, 8, 4, 64
QW, QKV = 512, 768
ROWS = 32
PIECE = QKV + QW + 16
SPLIT = 640
HALVES = (slice(0, SPLIT), slice(SPLIT, PIECE))
MESH = pl.DeviceIdType.MESH


def nn(a, b):
    return jnp.dot(a, b, preferred_element_type=F32)


def nt(a, b):
    return lax.dot_general(a, b, (((1,), (1,)), ((), ())), preferred_element_type=F32)


def norm_rows(x, gain, normed, inverse):
    for step in range(SEQ // ROWS):
        rows = slice(step * ROWS, step * ROWS + ROWS)
        xf = x(rows)
        inv = lax.rsqrt(jnp.mean(xf * xf, axis=1, keepdims=True) + EPSILON)
        normed[rows, :] = (xf * inv * gain[...]).astype(BF16)
        inverse[rows, :] = jnp.broadcast_to(inv, (ROWS, 128))


def forward(offset, normed, qkv, keep):
    proj_t, keys, values, soft, soft_low, att_t = keep
    for n in range(3):
        cols = slice(n * 256, n * 256 + 256)
        part = nn(normed[...], qkv[:, cols])
        proj_t[cols, :] = part.T.astype(BF16)
        if n == 2:
            low = part.astype(BF16)
            keys[0], keys[1] = low[:, :64], low[:, 64:128]
            values[0], values[1] = low[:, 128:192], low[:, 192:256]
    for head in range(HEADS):
        group = head // GROUP
        rows = slice(head * HD, head * HD + HD)
        scores = nn(keys[group], proj_t[rows, :])
        for half, depth in ((0, 128), (1, 256)):
            cols = slice(half * 128, half * 128 + 128)
            at_key = lax.broadcasted_iota(jnp.int32, (depth, 128), 0)
            at_query = lax.broadcasted_iota(jnp.int32, (depth, 128), 1) + half * 128
            allowed = (at_key <= at_query) & ((at_query < offset) | (at_key >= offset))
            part = jnp.where(allowed, scores[:depth, cols] * (HD**-0.5), -1e30)
            raised = jnp.exp(part - jnp.max(part, axis=0, keepdims=True))
            weights = raised * (1.0 / jnp.sum(raised, axis=0, keepdims=True))
            soft[head, :depth, cols] = weights
            soft_low[head, :depth, cols] = weights.astype(BF16)
        soft_low[head, 128:, :128] = jnp.zeros((128, 128), BF16)
        value_rows = slice(QW + 128 + group * HD, QW + 128 + group * HD + HD)
        att_t[rows, :] = nn(proj_t[value_rows, :], soft_low[head]).astype(BF16)


def backward(x, gain, inverse, qkv, outproj, upstream, keep, work, grad_t, gain_sum, result, midway=None):
    proj_t, keys, values, soft, soft_low, _ = keep
    att_grad, score_grad, grad, normed_grad = work
    for m in range(2):
        rows = slice(m * 256, m * 256 + 256)
        att_grad[rows, :] = nt(outproj[rows, :], upstream[...]).astype(BF16)
    for group in range(HEADS // GROUP):
        key_sum = jnp.zeros((HD, SEQ), F32)
        value_sum = jnp.zeros((HD, SEQ), F32)
        key_rows = slice(QW + group * HD, QW + group * HD + HD)
        value_rows = slice(QW + 128 + group * HD, QW + 128 + group * HD + HD)
        for head in range(group * GROUP, group * GROUP + GROUP):
            rows = slice(head * HD, head * HD + HD)
            low = att_grad[rows, :]
            soft_grad = nn(values[group], low)
            for half, depth in ((0, 128), (1, 256)):
                cols = slice(half * 128, half * 128 + 128)
                weights = soft[head, :depth, cols]
                part = soft_grad[:depth, cols]
                total = jnp.sum(weights * part, axis=0, keepdims=True)
                score_grad[head, :depth, cols] = (weights * (part - total) * (HD**-0.5)).astype(BF16)
            score_grad[head, 128:, :128] = jnp.zeros((128, 128), BF16)
            grad_t[rows, :] = nn(proj_t[key_rows, :], score_grad[head]).astype(BF16)
            key_sum = key_sum + nt(proj_t[rows, :], score_grad[head])
            value_sum = value_sum + nt(low, soft_low[head])
        grad_t[key_rows, :] = key_sum.astype(BF16)
        grad_t[value_rows, :] = value_sum.astype(BF16)
    if midway is not None:
        midway()
    for n in range(3):
        cols = slice(n * 256, n * 256 + 256)
        grad[:, cols] = grad_t[cols, :].T
    for n in range(4):
        cols = slice(n * 256, n * 256 + 256)
        normed_grad[:, cols] = nt(grad[...], qkv[cols, :])
    for step in range(SEQ // ROWS):
        rows = slice(step * ROWS, step * ROWS + ROWS)
        inv = inverse[rows, :][:, :1]
        scaled = x(rows) * inv
        hat = normed_grad[rows, :]
        both = hat * scaled
        partial = both[:8]
        for k in range(1, ROWS // 8):
            partial = partial + both[k * 8 : k * 8 + 8]
        gain_sum[...] += partial
        mean = jnp.mean(both * gain[...], axis=1, keepdims=True)
        moved = inv * (hat * gain[...] - scaled * mean)
        result[rows, :] = (upstream[rows, :].astype(F32) + moved).astype(BF16)


def weight_terms(q, grad_t, normed, att_t, upstream, gain_sum, piece):
    cols = pl.ds(pl.multiple_of(q * 256, 256), 256)
    for m in range(3):
        rows = slice(m * 256, m * 256 + 256)
        part = nn(grad_t[0][rows, :], normed[0][:, cols]) + nn(grad_t[1][rows, :], normed[1][:, cols])
        for core in range(2):
            piece[core, rows, :] = part[:, core * 128 : core * 128 + 128].astype(BF16)
    heads = pl.ds(pl.multiple_of(q * 128, 128), 128)
    for n in range(4):
        wide = slice(n * 256, n * 256 + 256)
        part = nn(att_t[0][heads, :], upstream[0][:, wide]) + nn(att_t[1][heads, :], upstream[1][:, wide])
        for core in range(2):
            for k in range(2):
                at = QKV + (2 * n + k) * HD
                block = part[core * HD : core * HD + HD, k * 128 : k * 128 + 128]
                piece[core, at : at + HD, :] = block.astype(BF16)
    for core in range(2):
        lanes = pl.ds(pl.multiple_of(q * 256 + core * 128, 128), 128)
        row = jnp.sum(gain_sum[:, lanes], axis=0, keepdims=True)
        piece[core, QKV + QW :, :] = jnp.broadcast_to(row, (16, 128)).astype(BF16)


SCRATCH = {
    "acts": pltpu.VMEM((2, 2, SEQ, D), BF16),
    "tops": pltpu.VMEM((2, SEQ, D), BF16),
    "seeds": pltpu.VMEM((2, SEQ, D), BF16),
    "gains": pltpu.VMEM((2, 1, D), F32),
    "qkvs": pltpu.VMEM((2, D, QKV), BF16),
    "outs": pltpu.VMEM((2, QW, D), BF16),
    "taken": pltpu.VMEM((2, SEQ, D), BF16),
    "grads": pltpu.VMEM((2, 2, SEQ, D), BF16),
    "normed": pltpu.VMEM((2, 2, SEQ, D), BF16),
    "grad_t": pltpu.VMEM((2, 2, QKV, SEQ), BF16),
    "att_t": pltpu.VMEM((2, 2, QW, SEQ), BF16),
    "gain_sum": pltpu.VMEM((2, 8, D), F32),
    "inverse": pltpu.VMEM((2, SEQ, 128), F32),
    "proj_t": pltpu.VMEM((2, QKV, SEQ), BF16),
    "keys": pltpu.VMEM((2, 2, SEQ, HD), BF16),
    "values": pltpu.VMEM((2, 2, SEQ, HD), BF16),
    "soft": pltpu.VMEM((2, HEADS, SEQ, SEQ), F32),
    "soft_low": pltpu.VMEM((2, HEADS, SEQ, SEQ), BF16),
    "att_grad": pltpu.VMEM((QW, SEQ), BF16),
    "score_grad": pltpu.VMEM((HEADS, SEQ, SEQ), BF16),
    "grad": pltpu.VMEM((SEQ, QKV), BF16),
    "normed_grad": pltpu.VMEM((SEQ, D), F32),
    "pieces": pltpu.VMEM((2, 4, 2, PIECE, 128), BF16),
    "paired": pltpu.VMEM((2, 4, PIECE, 128), BF16),
    "own": pltpu.VMEM((2, 4, PIECE, 128), BF16),
    "mirror": pltpu.VMEM((4, PIECE, 128), BF16),
    "ring": pltpu.VMEM((2, 4, PIECE, 128), BF16),
    "load_sem": pltpu.SemaphoreType.DMA((6, 2)),
    "save_sem": pltpu.SemaphoreType.DMA((2, 2)),
    "shift_sem": pltpu.SemaphoreType.DMA((2, 2)),
    "pair_sem": pltpu.SemaphoreType.DMA((2, 2, 4)),
    "mirror_sem": pltpu.SemaphoreType.DMA((2, 4, 2)),
    "ring_sem": pltpu.SemaphoreType.DMA((2, 2, 4, 2)),
}
LOADS = ("acts", "tops", "gains", "qkvs", "outs", "seeds")
AHEAD = ((0, 0), (1, 3), (0, 3))
BEHIND = ((0, 1), (1, 1), (0, 2))


def window(*refs):
    orders, offsets = refs[:2]
    sources = refs[2:14]
    input_grads, grad_gain, grad_qkv, grad_out = refs[14:18]
    s = dict(zip(SCRATCH, refs[18:]))

    section, replica = lax.axis_index("section"), lax.axis_index("dp")
    sections, replicas = lax.axis_size("section"), lax.axis_size("dp")
    low, core = section % 2, replica % 2
    height = (replica // 2) * 2 + low
    partner = (section, replica + 1 - 2 * core)
    across = (sections - 2 - section + 2 * low, replica)
    above = (section + 1 - 2 * low, (replica + 2 * low) % replicas)
    below = (section + 1 - 2 * low, (replica + replicas - 2 + 2 * low) % replicas)
    later = ((section + 1) % sections, replica)
    sooner = ((section + sections - 1) % sections, replica)

    barrier = pltpu.get_barrier_semaphore()
    for peer in (partner, across, above, below, later, sooner):
        pl.semaphore_signal(barrier, inc=1, device_id=peer, device_id_type=MESH)

    def load(name, c):
        where = LOADS.index(name)
        return pltpu.make_async_copy(sources[2 * where + c], s[name].at[pl.ds(c, 1)], s["load_sem"].at[where, c])

    for c in range(2):
        for name in ("acts", "gains", "qkvs", "outs", "tops"):
            load(name, c).start()
    for c in range(2):
        load("seeds", c).start()

    def loaded(name, c):
        where = s[name].at[pl.ds(c, 1)]
        pltpu.make_async_copy(where, where, s["load_sem"].at[LOADS.index(name), c]).wait()

    def picked(c, slot):
        chosen = orders[(1 - c) * 2 + slot]
        offset = jnp.where(chosen == 0, offsets[(1 - c) * 2], offsets[(1 - c) * 2 + 1])

        def rows_of(rows):
            return jnp.where(chosen == 0, s["acts"][c, 0, rows, :].astype(F32), s["acts"][c, 1, rows, :].astype(F32))

        return rows_of, offset

    def keep(c, slot):
        names = ("proj_t", "keys", "values", "soft", "soft_low")
        return (*(s[name].at[c] for name in names), s["att_t"].at[c, slot])

    def run_forward(c, slot):
        x, offset = picked(c, slot)
        norm_rows(x, s["gains"].at[c], s["normed"].at[c, slot], s["inverse"].at[c])
        forward(offset, s["normed"].at[c, slot], s["qkvs"].at[c], keep(c, slot))

    def run_backward(c, slot, upstream, midway=None):
        work = tuple(s[name] for name in ("att_grad", "score_grad", "grad", "normed_grad"))
        backward(
            picked(c, slot)[0], s["gains"].at[c], s["inverse"].at[c], s["qkvs"].at[c], s["outs"].at[c],
            upstream, keep(c, slot), work, s["grad_t"].at[c, slot], s["gain_sum"].at[c],
            s["grads"].at[c, slot], midway,
        )

    def save(c, slot):
        return pltpu.make_async_copy(
            s["grads"].at[c, slot], input_grads.at[1 - c, 0, slot], s["save_sem"].at[c, slot]
        )

    def remote(source, target, sems, device):
        return pltpu.make_async_remote_copy(
            src_ref=source, dst_ref=target, send_sem=sems[0], recv_sem=sems[1],
            device_id=device, device_id_type=MESH,
        )

    def shift(c):
        peer = ((section + sections + 1 - 2 * c) % sections, replica)
        sems = (s["shift_sem"].at[0, c], s["shift_sem"].at[1, c])
        return remote(s["grads"].at[c, 0], s["taken"].at[c], sems, peer)

    def pair(c, j):
        sems = (s["pair_sem"].at[0, c, j], s["pair_sem"].at[1, c, j])
        return remote(s["pieces"].at[c, j, 1 - core], s["paired"].at[c, j], sems, partner)

    def fold(j, h):
        sems = (s["mirror_sem"].at[0, j, h], s["mirror_sem"].at[1, j, h])
        return remote(s["own"].at[0, j, HALVES[h]], s["mirror"].at[j, HALVES[h]], sems, across)

    def add_pair(c, j, rows):
        total = s["pieces"][c, j, core, rows, :].astype(F32) + s["paired"][c, j, rows, :].astype(F32)
        s["own"][c, j, rows, :] = total.astype(BF16)

    def send_mirror():
        for j in (0, 1, 3, 2):
            pair(0, j).wait_recv()
            for h in range(2):
                add_pair(0, j, HALVES[h])
        for first, second in ((0, 1), (3, 2)):
            for j, h in ((first, 1), (second, 0), (first, 0), (second, 1)):
                fold(j, h).start()

    s["gain_sum"][...] = jnp.zeros_like(s["gain_sum"])

    @pl.loop(0, 2)
    def _(c):
        for name in ("acts", "gains", "qkvs"):
            loaded(name, c)
        run_forward(c, 0)
        loaded("outs", c)
        loaded("tops", c)
        run_backward(c, 0, s["tops"].at[c])

        @pl.when(c == 0)
        def _():
            pl.semaphore_wait(barrier, 6)

        shift(c).start()
        save(c, 0).start()

    @pl.loop(0, 2)
    def _(c):
        run_forward(c, 1)

    @pl.loop(0, 2)
    def _(c):
        loaded("seeds", c)
        shift(c).wait_recv()

        @pl.when(section == (sections - 1) * c)
        def _():
            s["taken"][c] = s["seeds"][c]

        def midway():
            @pl.when(c == 1)
            def _():
                send_mirror()

        run_backward(c, 1, s["taken"].at[c], midway)
        save(c, 1).start()

        @pl.loop(0, 4)
        def _(j):
            weight_terms(
                ((height + 3 + c + 2 * j) % replicas) // 2,
                [s["grad_t"].at[c, k] for k in range(2)],
                [s["normed"].at[c, k] for k in range(2)],
                [s["att_t"].at[c, k] for k in range(2)],
                [s["tops"].at[c], s["taken"].at[c]],
                s["gain_sum"].at[c],
                s["pieces"].at[c, j],
            )
            pair(c, j).start()

    ways = (above, below)

    def term(way, step):
        if step == 0:
            return s["own"].at[1, 0]
        mirrored, j = (AHEAD, BEHIND)[way][step - 1]
        return s["mirror"].at[j] if mirrored == 0 else s["own"].at[1, j]

    def hop(way, step, h):
        sems = (s["ring_sem"].at[0, way, step, h], s["ring_sem"].at[1, way, step, h])
        return remote(term(way, step).at[HALVES[h]], s["ring"].at[way, step, HALVES[h]], sems, ways[way])

    def forward_on(way, step, h):
        rows = HALVES[h]
        if step > 0:
            mirrored, j = (AHEAD, BEHIND)[way][step - 1]
            if mirrored == 0:
                fold(j, h).wait_recv()
            if step > 1 or h == way:
                hop(way, step - 1, h).wait_recv()
                mine = term(way, step)
                total = mine[rows, :].astype(F32) + s["ring"][way, step - 1, rows, :].astype(F32)
                mine[rows, :] = total.astype(BF16)
        hop(way, step, h).start()

    pair(1, 0).wait_recv()
    for h in range(2):
        add_pair(1, 0, HALVES[h])
        forward_on(h, 0, h)
    for j in (3, 1, 2):
        pair(1, j).wait_recv()
        for h in range(2):
            add_pair(1, j, HALVES[h])
    for step in range(1, 4):
        for turn in range(2):
            for way in range(2):
                forward_on(way, step, (1 - way) if turn == 0 else way)
    for way in range(2):
        for h in range(2):
            hop(way, 3, h).wait_recv()

    total = s["own"][1, 2].astype(F32) + s["ring"][0, 3].astype(F32) + s["ring"][1, 3].astype(F32)
    for n in range(3):
        grad_qkv[0, :, n * 256 : n * 256 + 256] = total[n * 256 : n * 256 + 256, :].T
    for k in range(8):
        grad_out[0, :, k * 128 : k * 128 + 128] = total[QKV + k * HD : QKV + k * HD + HD, :]
    grad_gain[...] = total[QKV + QW : QKV + QW + 1, :]

    for c in range(2):
        shift(c).wait_send()
        for slot in range(2):
            save(c, slot).wait()
        for j in range(4):
            pair(c, j).wait_send()
    for j in range(4):
        for h in range(2):
            fold(j, h).wait_send()
    for way in range(2):
        hop(way, 0, way).wait_send()
        for step in range(1, 4):
            for h in range(2):
                hop(way, step, h).wait_send()


def shards(
    act_down, act_up, grad_down, grad_up, seed_down, seed_up, gain_down, qkv_down, outproj_down,
    gain_up, qkv_up, outproj_up, doc_offsets, slot_order,
):
    shapes = (
        jax.ShapeDtypeStruct((2, 1, 2, SEQ, D), BF16),
        jax.ShapeDtypeStruct((1, 128), F32),
        jax.ShapeDtypeStruct((1, 128, QKV), F32),
        jax.ShapeDtypeStruct((1, HD, D), F32),
    )
    whole = pl.BlockSpec(memory_space=pltpu.VMEM)
    anywhere = pl.BlockSpec(memory_space=pl.ANY)
    numbers = pl.BlockSpec(memory_space=pltpu.SMEM)
    return pl.pallas_call(
        window,
        in_specs=[numbers] * 2 + [anywhere] * 12,
        out_specs=[anywhere, whole, whole, whole],
        out_shape=shapes,
        scratch_shapes=list(SCRATCH.values()),
        compiler_params=pltpu.CompilerParams(
            vmem_limit_bytes=60 * 2**20, collective_id=0, has_side_effects=True
        ),
    )(
        slot_order.reshape(4), doc_offsets.reshape(4), act_up, act_down, grad_up, grad_down,
        gain_up[None], gain_down[None], qkv_up, qkv_down, outproj_up, outproj_down, seed_up[None], seed_down[None],
    )


def solution(mesh):
    return jax.shard_map(
        shards,
        mesh=mesh,
        in_specs=(
            P("section", None, "dp", None),
            P("section", None, "dp", None),
            P("section", "dp", None),
            P("section", "dp", None),
            P("dp", None),
            P("dp", None),
            P("section", None),
            P("section", None, None),
            P("section", None, None),
            P("section", None),
            P("section", None, None),
            P("section", None, None),
            P(None, "section", None, "dp"),
            P(None, "section", None),
        ),
        out_specs=(
            P(None, "section", None, "dp", None),
            P("section", "dp"),
            P("section", "dp", None),
            P("section", "dp", None),
        ),
        check_vma=False,
    )
```

```python
import functools

import jax
import jax.numpy as jnp
from jax import lax
from jax.experimental import pallas as pl
from jax.experimental.pallas import tpu as pltpu
from jax.sharding import PartitionSpec as P

F32, BF16 = jnp.float32, jnp.bfloat16
EPSILON = 1e-05
D, SEQ, HEADS, GROUP, HD = 1024, 256, 8, 4, 64
QW, QKV = 512, 768
ROWS = 32
PIECE = QKV + QW + 16
BLOCKS = (slice(0, QW), slice(QW, PIECE))
FOLDS = (slice(0, QW), slice(QW, 896), slice(896, PIECE))
PARTS = (slice(0, 256), slice(256, QW), slice(QW, 896), slice(896, PIECE))
FOLD_OF = (0, 0, 1, 2)
MESH = pl.DeviceIdType.MESH


def nn(a, b):
    return jnp.dot(a, b, preferred_element_type=F32)


def nt(a, b):
    return lax.dot_general(a, b, (((1,), (1,)), ((), ())), preferred_element_type=F32)


def norm_rows(x, gain, normed, inverse):
    for step in range(SEQ // ROWS):
        rows = slice(step * ROWS, step * ROWS + ROWS)
        xf = x(rows)
        inv = lax.rsqrt(jnp.mean(xf * xf, axis=1, keepdims=True) + EPSILON)
        normed[rows, :] = (xf * inv * gain[...]).astype(BF16)
        inverse[rows, :] = jnp.broadcast_to(inv, (ROWS, 128))


def forward(offset, normed, qkv, keep):
    proj_t, keys, values, soft, soft_low, att_t = keep
    for n in range(3):
        cols = slice(n * 256, n * 256 + 256)
        part = nn(normed[...], qkv[:, cols])
        proj_t[cols, :] = part.T.astype(BF16)
        if n == 2:
            low = part.astype(BF16)
            keys[0], keys[1] = low[:, :64], low[:, 64:128]
            values[0], values[1] = low[:, 128:192], low[:, 192:256]
    for head in range(HEADS):
        group = head // GROUP
        rows = slice(head * HD, head * HD + HD)
        scores = nn(keys[group], proj_t[rows, :])
        for half, depth in ((0, 128), (1, 256)):
            cols = slice(half * 128, half * 128 + 128)
            at_key = lax.broadcasted_iota(jnp.int32, (depth, 128), 0)
            at_query = lax.broadcasted_iota(jnp.int32, (depth, 128), 1) + half * 128
            allowed = (at_key <= at_query) & ((at_query < offset) | (at_key >= offset))
            part = jnp.where(allowed, scores[:depth, cols] * (HD**-0.5), -1e30)
            raised = jnp.exp(part - jnp.max(part, axis=0, keepdims=True))
            weights = raised * (1.0 / jnp.sum(raised, axis=0, keepdims=True))
            soft[head, :depth, cols] = weights
            soft_low[head, :depth, cols] = weights.astype(BF16)
        soft_low[head, 128:, :128] = jnp.zeros((128, 128), BF16)
        value_rows = slice(QW + 128 + group * HD, QW + 128 + group * HD + HD)
        att_t[rows, :] = nn(proj_t[value_rows, :], soft_low[head]).astype(BF16)


def backward(x, gain, inverse, qkv, outproj, upstream, keep, work, grad_t, gain_sum, result, hooks=()):
    hooks = dict(hooks)
    proj_t, keys, values, soft, soft_low, _ = keep
    att_grad, score_grad, grad, normed_grad = work
    for m in range(2):
        rows = slice(m * 256, m * 256 + 256)
        att_grad[rows, :] = nt(outproj[rows, :], upstream[...]).astype(BF16)
    if "start" in hooks:
        hooks["start"]()
    for group in range(HEADS // GROUP):
        key_sum = jnp.zeros((HD, SEQ), F32)
        value_sum = jnp.zeros((HD, SEQ), F32)
        key_rows = slice(QW + group * HD, QW + group * HD + HD)
        value_rows = slice(QW + 128 + group * HD, QW + 128 + group * HD + HD)
        for head in range(group * GROUP, group * GROUP + GROUP):
            rows = slice(head * HD, head * HD + HD)
            low = att_grad[rows, :]
            soft_grad = nn(values[group], low)
            for half, depth in ((0, 128), (1, 256)):
                cols = slice(half * 128, half * 128 + 128)
                weights = soft[head, :depth, cols]
                part = soft_grad[:depth, cols]
                total = jnp.sum(weights * part, axis=0, keepdims=True)
                score_grad[head, :depth, cols] = (weights * (part - total) * (HD**-0.5)).astype(BF16)
            score_grad[head, 128:, :128] = jnp.zeros((128, 128), BF16)
            grad_t[rows, :] = nn(proj_t[key_rows, :], score_grad[head]).astype(BF16)
            key_sum = key_sum + nt(proj_t[rows, :], score_grad[head])
            value_sum = value_sum + nt(low, soft_low[head])
        grad_t[key_rows, :] = key_sum.astype(BF16)
        grad_t[value_rows, :] = value_sum.astype(BF16)
        if group in hooks:
            hooks[group]()
    for n in range(3):
        cols = slice(n * 256, n * 256 + 256)
        grad[:, cols] = grad_t[cols, :].T
    for n in range(4):
        cols = slice(n * 256, n * 256 + 256)
        normed_grad[:, cols] = nt(grad[...], qkv[cols, :])
    for step in range(SEQ // ROWS):
        rows = slice(step * ROWS, step * ROWS + ROWS)
        inv = inverse[rows, :][:, :1]
        scaled = x(rows) * inv
        hat = normed_grad[rows, :]
        both = hat * scaled
        partial = both[:8]
        for k in range(1, ROWS // 8):
            partial = partial + both[k * 8 : k * 8 + 8]
        gain_sum[...] += partial
        mean = jnp.mean(both * gain[...], axis=1, keepdims=True)
        moved = inv * (hat * gain[...] - scaled * mean)
        result[rows, :] = (upstream[rows, :].astype(F32) + moved).astype(BF16)


def out_terms(q, att_t, upstream, piece):
    heads = pl.ds(pl.multiple_of(q * 128, 128), 128)
    for n in range(4):
        wide = slice(n * 256, n * 256 + 256)
        part = nn(att_t[0][heads, :], upstream[0][:, wide]) + nn(att_t[1][heads, :], upstream[1][:, wide])
        for core in range(2):
            for k in range(2):
                at = (2 * n + k) * HD
                block = part[core * HD : core * HD + HD, k * 128 : k * 128 + 128]
                piece[core, at : at + HD, :] = block.astype(BF16)


def qkv_terms(q, grad_t, normed, gain_sum, piece):
    cols = pl.ds(pl.multiple_of(q * 256, 256), 256)
    for m in range(3):
        rows = slice(m * 256, m * 256 + 256)
        part = nn(grad_t[0][rows, :], normed[0][:, cols]) + nn(grad_t[1][rows, :], normed[1][:, cols])
        for core in range(2):
            at = QW + m * 256
            piece[core, at : at + 256, :] = part[:, core * 128 : core * 128 + 128].astype(BF16)
    for core in range(2):
        lanes = pl.ds(pl.multiple_of(q * 256 + core * 128, 128), 128)
        row = jnp.sum(gain_sum[:, lanes], axis=0, keepdims=True)
        piece[core, QW + QKV :, :] = jnp.broadcast_to(row, (16, 128)).astype(BF16)


SCRATCH = {
    "orders": pltpu.SMEM((2, 1, 2), jnp.int32),
    "offsets": pltpu.SMEM((2, 1, 1, 2), jnp.int32),
    "number_sem": pltpu.SemaphoreType.DMA((2,)),
    "acts": pltpu.VMEM((2, 2, SEQ, D), BF16),
    "tops": pltpu.VMEM((2, SEQ, D), BF16),
    "seeds": pltpu.VMEM((2, SEQ, D), BF16),
    "gains": pltpu.VMEM((2, 1, D), F32),
    "qkvs": pltpu.VMEM((2, D, QKV), BF16),
    "outs": pltpu.VMEM((2, QW, D), BF16),
    "taken": pltpu.VMEM((2, SEQ, D), BF16),
    "normed": pltpu.VMEM((2, 2, SEQ, D), BF16),
    "grad_t": pltpu.VMEM((2, 2, QKV, SEQ), BF16),
    "att_t": pltpu.VMEM((2, 2, QW, SEQ), BF16),
    "gain_sum": pltpu.VMEM((2, 8, D), F32),
    "inverse": pltpu.VMEM((2, SEQ, 128), F32),
    "proj_t": pltpu.VMEM((2, QKV, SEQ), BF16),
    "keys": pltpu.VMEM((2, 2, SEQ, HD), BF16),
    "values": pltpu.VMEM((2, 2, SEQ, HD), BF16),
    "soft": pltpu.VMEM((2, HEADS, SEQ, SEQ), F32),
    "soft_low": pltpu.VMEM((2, HEADS, SEQ, SEQ), BF16),
    "att_grad": pltpu.VMEM((QW, SEQ), BF16),
    "score_grad": pltpu.VMEM((HEADS, SEQ, SEQ), BF16),
    "grad": pltpu.VMEM((SEQ, QKV), BF16),
    "normed_grad": pltpu.VMEM((SEQ, D), F32),
    "pieces": pltpu.VMEM((2, 4, 2, PIECE, 128), BF16),
    "paired": pltpu.VMEM((2, 4, PIECE, 128), BF16),
    "own": pltpu.VMEM((2, 4, PIECE, 128), BF16),
    "mirror": pltpu.VMEM((4, PIECE, 128), BF16),
    "ring": pltpu.VMEM((2, 4, PIECE, 128), BF16),
    "load_sem": pltpu.SemaphoreType.DMA((6, 2)),
    "shift_sem": pltpu.SemaphoreType.DMA((2, 2)),
    "pair_sem": pltpu.SemaphoreType.DMA((2, 2, 2, 4)),
    "fold_sem": pltpu.SemaphoreType.DMA((2, 3, 4)),
    "ring_sem": pltpu.SemaphoreType.DMA((2, 2, 4, 4)),
}
VMEM_MB = 44
LOADS = ("acts", "tops", "gains", "qkvs", "outs", "seeds")
AHEAD = ((0, 0), (1, 3), (0, 3))
BEHIND = ((0, 1), (1, 1), (0, 2))


def window(*refs):
    sources = refs[2:14]
    grads, grad_gain, grad_qkv, grad_out = refs[14:18]
    s = dict(zip(SCRATCH, refs[18:]))
    orders, offsets = s["orders"], s["offsets"]
    numbers = [
        pltpu.make_async_copy(refs[k], into, s["number_sem"].at[k]) for k, into in enumerate((orders, offsets))
    ]
    for copy in numbers:
        copy.start()

    section, replica = lax.axis_index("section"), lax.axis_index("dp")
    sections, replicas = lax.axis_size("section"), lax.axis_size("dp")
    low, core = section % 2, replica % 2
    height = (replica // 2) * 2 + low
    partner = (section, replica + 1 - 2 * core)
    across = (sections - 2 - section + 2 * low, replica)
    ways = (
        (section + 1 - 2 * low, (replica + 2 * low) % replicas),
        (section + 1 - 2 * low, (replica + replicas - 2 + 2 * low) % replicas),
    )
    nexts = (((section + 1) % sections, replica), ((section + sections - 1) % sections, replica))

    barrier = pltpu.get_barrier_semaphore()
    for peer in (partner, across, *ways, *nexts):
        pl.semaphore_signal(barrier, inc=1, device_id=peer, device_id_type=MESH)

    def load(name, c):
        where = LOADS.index(name)
        return pltpu.make_async_copy(sources[2 * where + c], s[name].at[pl.ds(c, 1)], s["load_sem"].at[where, c])

    def picked(c, slot):
        chosen = orders[1 - c, 0, slot]
        offset = jnp.where(chosen == 0, offsets[1 - c, 0, 0, 0], offsets[1 - c, 0, 0, 1])

        def rows_of(rows):
            return jnp.where(chosen == 0, s["acts"][c, 0, rows, :].astype(F32), s["acts"][c, 1, rows, :].astype(F32))

        return rows_of, offset

    def keep(c, slot):
        names = ("proj_t", "keys", "values", "soft", "soft_low")
        return (*(s[name].at[c] for name in names), s["att_t"].at[c, slot])

    def run_norm(c, slot):
        norm_rows(picked(c, slot)[0], s["gains"].at[c], s["normed"].at[c, slot], s["inverse"].at[c])

    def run_forward(c, slot):
        forward(picked(c, slot)[1], s["normed"].at[c, slot], s["qkvs"].at[c], keep(c, slot))

    def run_backward(c, slot, upstream, hooks=()):
        work = tuple(s[name] for name in ("att_grad", "score_grad", "grad", "normed_grad"))
        backward(
            picked(c, slot)[0], s["gains"].at[c], s["inverse"].at[c], s["qkvs"].at[c], s["outs"].at[c],
            upstream, keep(c, slot), work, s["grad_t"].at[c, slot], s["gain_sum"].at[c],
            grads.at[1 - c, 0, slot], hooks,
        )

    def remote(source, target, sems, device):
        return pltpu.make_async_remote_copy(
            src_ref=source, dst_ref=target, send_sem=sems[0], recv_sem=sems[1],
            device_id=device, device_id_type=MESH,
        )

    def shift(c):
        sems = (s["shift_sem"].at[0, c], s["shift_sem"].at[1, c])
        return remote(grads.at[1 - c, 0, 0], s["taken"].at[c], sems, nexts[c])

    def pair(c, b, j):
        sems = (s["pair_sem"].at[0, c, b, j], s["pair_sem"].at[1, c, b, j])
        rows = BLOCKS[b]
        return remote(s["pieces"].at[c, j, 1 - core, rows], s["paired"].at[c, j, rows], sems, partner)

    def fold(f, j):
        sems = (s["fold_sem"].at[0, f, j], s["fold_sem"].at[1, f, j])
        rows = FOLDS[f]
        return remote(s["own"].at[0, j, rows], s["mirror"].at[j, rows], sems, across)

    def add_pair(c, b, j):
        rows = BLOCKS[b]
        pair(c, b, j).wait_recv()
        total = s["pieces"][c, j, core, rows, :].astype(F32) + s["paired"][c, j, rows, :].astype(F32)
        s["own"][c, j, rows, :] = total.astype(BF16)

    def chip(c, j):
        return ((height + 3 + c + 2 * j) % replicas) // 2

    def take(c):
        load("seeds", c).wait()
        shift(c).wait_recv()

        @pl.when(section == (sections - 1) * c)
        def _():
            s["taken"][c] = s["seeds"][c]

    def make_out_terms(c):
        @pl.loop(0, 4)
        def _(j):
            att_t = [s["att_t"].at[c, k] for k in range(2)]
            out_terms(chip(c, j), att_t, [s["tops"].at[c], s["taken"].at[c]], s["pieces"].at[c, j])
            pair(c, 0, j).start()

    def make_qkv_terms(c):
        @pl.loop(0, 4)
        def _(j):
            grad_t, normed = ([s[name].at[c, k] for k in range(2)] for name in ("grad_t", "normed"))
            qkv_terms(chip(c, j), grad_t, normed, s["gain_sum"].at[c], s["pieces"].at[c, j])
            pair(c, 1, j).start()

    def send_out_folds():
        for j in (0, 1, 3, 2):
            add_pair(0, 0, j)
            fold(0, j).start()

    def send_qkv_folds():
        for first, second in ((0, 1), (3, 2)):
            for j in (first, second):
                add_pair(0, 1, j)
            for j, f in ((first, 2), (second, 1), (first, 1), (second, 2)):
                fold(f, j).start()

    def term(way, step):
        if step == 0:
            return s["own"].at[1, 0]
        mirrored, j = (AHEAD, BEHIND)[way][step - 1]
        return s["mirror"].at[j] if mirrored == 0 else s["own"].at[1, j]

    def hop(way, step, p):
        sems = (s["ring_sem"].at[0, way, step, p], s["ring_sem"].at[1, way, step, p])
        return remote(term(way, step).at[PARTS[p]], s["ring"].at[way, step, PARTS[p]], sems, ways[way])

    folded = set()

    def send_on(way, step, p):
        rows = PARTS[p]
        if step > 0:
            mirrored, j = (AHEAD, BEHIND)[way][step - 1]
            if mirrored == 0 and (FOLD_OF[p], j) not in folded:
                folded.add((FOLD_OF[p], j))
                fold(FOLD_OF[p], j).wait_recv()
            if step > 1 or p % 2 == way:
                hop(way, step - 1, p).wait_recv()
                mine = term(way, step)
                total = mine[rows, :].astype(F32) + s["ring"][way, step - 1, rows, :].astype(F32)
                mine[rows, :] = total.astype(BF16)
        hop(way, step, p).start()

    def ring_step(b, step):
        if step == 0:
            for way in range(2):
                send_on(way, 0, 2 * b + way)
            return
        for turn in range(2):
            for way in range(2):
                send_on(way, step, 2 * b + (1 - way if turn == 0 else way))

    def final(b):
        for way in range(2):
            for p in (2 * b, 2 * b + 1):
                hop(way, 3, p).wait_recv()
        rows = BLOCKS[b]
        return s["own"][1, 2, rows].astype(F32) + s["ring"][0, 3, rows].astype(F32) + s["ring"][1, 3, rows].astype(F32)

    def ring_out_start():
        for j in (0, 3, 1, 2):
            add_pair(1, 0, j)
        ring_step(0, 0)

    for c in range(2):
        for name in ("acts", "gains", "qkvs", "outs", "tops"):
            load(name, c).start()
    for c in range(2):
        load("seeds", c).start()
    s["gain_sum"][...] = jnp.zeros_like(s["gain_sum"])

    for copy in numbers:
        copy.wait()
    for c in range(2):
        load("acts", c).wait()
        load("gains", c).wait()
        run_norm(c, 0)
        load("qkvs", c).wait()
        run_forward(c, 0)
        load("outs", c).wait()
        load("tops", c).wait()
        run_backward(c, 0, s["tops"].at[c])
        if c == 0:
            pl.semaphore_wait(barrier, 6)
        shift(c).start()
    for c in range(2):
        run_norm(c, 1)
        run_forward(c, 1)

    take(0)
    make_out_terms(0)
    run_backward(0, 1, s["taken"].at[0], {0: send_out_folds})
    make_qkv_terms(0)
    take(1)
    make_out_terms(1)
    run_backward(1, 1, s["taken"].at[1], {"start": send_qkv_folds, 0: ring_out_start})
    ring_step(0, 1)
    make_qkv_terms(1)
    ring_step(0, 2)
    for j in (0, 3, 1, 2):
        add_pair(1, 1, j)
    ring_step(1, 0)
    ring_step(0, 3)
    for step in range(1, 4):
        ring_step(1, step)

    total = final(0)
    for k in range(8):
        grad_out[0, :, k * 128 : k * 128 + 128] = total[k * HD : k * HD + HD, :]
    total = final(1)
    for n in range(3):
        grad_qkv[0, :, n * 256 : n * 256 + 256] = total[n * 256 : n * 256 + 256, :].T
    grad_gain[...] = total[QKV : QKV + 1, :]

    for c in range(2):
        shift(c).wait_send()
        for b in range(2):
            for j in range(4):
                pair(c, b, j).wait_send()
    for j in range(4):
        for f in range(3):
            fold(f, j).wait_send()
    for way in range(2):
        for step in range(4):
            for p in range(4):
                if step > 0 or p % 2 == way:
                    hop(way, step, p).wait_send()


def shards(
    act_down, act_up, grad_down, grad_up, seed_down, seed_up, gain_down, qkv_down, outproj_down,
    gain_up, qkv_up, outproj_up, doc_offsets, slot_order,
):
    shapes = (
        jax.ShapeDtypeStruct((2, 1, 2, SEQ, D), BF16),
        jax.ShapeDtypeStruct((1, 128), F32),
        jax.ShapeDtypeStruct((1, 128, QKV), F32),
        jax.ShapeDtypeStruct((1, HD, D), F32),
    )
    whole = pl.BlockSpec(memory_space=pltpu.VMEM)
    outside = pl.BlockSpec(memory_space=pltpu.HBM)
    return pl.pallas_call(
        window,
        in_specs=[outside] * 14,
        out_specs=[whole] * 4,
        out_shape=shapes,
        scratch_shapes=list(SCRATCH.values()),
        compiler_params=pltpu.CompilerParams(
            vmem_limit_bytes=VMEM_MB * 2**20, collective_id=0, has_side_effects=True
        ),
    )(
        *(
            pltpu.with_memory_space_constraint(x, pltpu.HBM)
            for x in (
                slot_order, doc_offsets.transpose(0, 1, 3, 2), act_up, act_down, grad_up, grad_down, gain_up[None], gain_down[None],
                qkv_up, qkv_down, outproj_up, outproj_down, seed_up[None], seed_down[None],
            )
        ),
    )


def solution(mesh):
    return jax.shard_map(
        shards,
        mesh=mesh,
        in_specs=(
            P("section", None, "dp", None),
            P("section", None, "dp", None),
            P("section", "dp", None),
            P("section", "dp", None),
            P("dp", None),
            P("dp", None),
            P("section", None),
            P("section", None, None),
            P("section", None, None),
            P("section", None),
            P("section", None, None),
            P("section", None, None),
            P(None, "section", None, "dp"),
            P(None, "section", None),
        ),
        out_specs=(
            P(None, "section", None, "dp", None),
            P("section", "dp"),
            P("section", "dp", None),
            P("section", "dp", None),
        ),
        check_vma=False,
    )
```

```python
import math

import jax
import jax.numpy as jnp
from jax import lax
from jax.experimental import pallas as pl
from jax.experimental.pallas import tpu as pltpu
from jax.sharding import PartitionSpec as P

F32, BF16 = jnp.float32, jnp.bfloat16
EPSILON = 1e-05
D, SEQ, HEADS, GROUP, HD = 1024, 256, 8, 4, 64
QW, QKV = 512, 768
ROWS = 32
PIECE = QKV + QW + 16
BLOCKS = (slice(0, QW), slice(QW, PIECE))
FOLDS = (slice(0, QW), slice(QW, 896), slice(896, PIECE))
PARTS = (slice(0, 256), slice(256, QW), slice(QW, 896), slice(896, PIECE))
FOLD_OF = (0, 0, 1, 2)
MESH = pl.DeviceIdType.MESH
SCALE = HD**-0.5
SCALE_2 = SCALE * math.log2(math.e)


def nn(a, b):
    return jnp.dot(a, b, preferred_element_type=F32)


def nt(a, b):
    return lax.dot_general(a, b, (((1,), (1,)), ((), ())), preferred_element_type=F32)


def stagger(stages):
    for step in range(HEADS + len(stages) - 1):
        for k, stage in enumerate(stages):
            if 0 <= step - k < HEADS:
                stage(step - k)


def norm_rows(x, gain, normed, inverse):
    for step in range(SEQ // ROWS):
        rows = slice(step * ROWS, step * ROWS + ROWS)
        xf = x(rows)
        inv = lax.rsqrt(jnp.mean(xf * xf, axis=1, keepdims=True) + EPSILON)
        normed[rows, :] = (xf * inv * gain[...]).astype(BF16)
        inverse[rows, :] = jnp.broadcast_to(inv, (ROWS, 128))


def set_ceiling(offset, ceiling):
    for half, depth in ((0, 128), (1, 256)):
        at_key = lax.broadcasted_iota(jnp.int32, (depth, 128), 0)
        at_query = lax.broadcasted_iota(jnp.int32, (depth, 128), 1) + half * 128
        allowed = (at_key <= at_query) & ((at_query < offset) | (at_key >= offset))
        ceiling[:depth, half * 128 : half * 128 + 128] = jnp.where(allowed, jnp.inf, -1e30)


def forward(ceiling, normed, qkv, keep):
    proj_t, keys, values, soft, soft_low, att_t = keep
    for n in range(3):
        cols = slice(n * 256, n * 256 + 256)
        part = nn(normed[...], qkv[:, cols])
        proj_t[cols, :] = part.T.astype(BF16)
        if n == 2:
            low = part.astype(BF16)
            keys[0], keys[1] = low[:, :64], low[:, 64:128]
            values[0], values[1] = low[:, 128:192], low[:, 192:256]
    def score(head):
        rows = slice(head * HD, head * HD + HD)
        soft[head] = nn(keys[head // GROUP], proj_t[rows, :])

    def normalize(head):
        for half, depth in ((0, 128), (1, 256)):
            cols = slice(half * 128, half * 128 + 128)
            part = jnp.minimum(soft[head, :depth, cols] * SCALE_2, ceiling[:depth, cols])
            raised = jnp.exp2(part - jnp.max(part, axis=0, keepdims=True))
            weights = raised * (1.0 / jnp.sum(raised, axis=0, keepdims=True))
            soft[head, :depth, cols] = weights
            soft_low[head, :depth, cols] = weights.astype(BF16)
        soft_low[head, 128:, :128] = jnp.zeros((128, 128), BF16)

    def attend(head):
        rows = slice(head * HD, head * HD + HD)
        value_rows = slice(QW + 128 + head // GROUP * HD, QW + 128 + head // GROUP * HD + HD)
        att_t[rows, :] = nn(proj_t[value_rows, :], soft_low[head]).astype(BF16)

    stagger((score, normalize, attend))


def backward(x, gain, inverse, qkv, outproj, upstream, keep, work, grad_t, gain_sum, result, hooks=()):
    hooks = dict(hooks)
    proj_t, keys, values, soft, soft_low, _ = keep
    att_grad, soft_grad, score_grad, grad, normed_grad = work
    for m in range(2):
        rows = slice(m * 256, m * 256 + 256)
        att_grad[rows, :] = nt(outproj[rows, :], upstream[...]).astype(BF16)
    if "start" in hooks:
        hooks["start"]()
    sums = [[None, None], [None, None]]

    def soften(head):
        rows = slice(head * HD, head * HD + HD)
        soft_grad[head % 4] = nn(values[head // GROUP], att_grad[rows, :])

    def combine(head):
        for half, depth in ((0, 128), (1, 256)):
            cols = slice(half * 128, half * 128 + 128)
            weights = soft[head, :depth, cols]
            part = soft_grad[head % 4, :depth, cols]
            total = jnp.sum(weights * part, axis=0, keepdims=True)
            score_grad[head, :depth, cols] = (weights * (part - total)).astype(BF16)
        score_grad[head, 128:, :128] = jnp.zeros((128, 128), BF16)

    def project(head):
        group = head // GROUP
        rows = slice(head * HD, head * HD + HD)
        key_rows = slice(QW + group * HD, QW + group * HD + HD)
        value_rows = slice(QW + 128 + group * HD, QW + 128 + group * HD + HD)
        grad_t[rows, :] = (nn(proj_t[key_rows, :], score_grad[head]) * SCALE).astype(BF16)
        for k, part in enumerate((nt(proj_t[rows, :], score_grad[head]), nt(att_grad[rows, :], soft_low[head]))):
            sums[group][k] = part if sums[group][k] is None else sums[group][k] + part
        if head % GROUP == GROUP - 1:
            grad_t[key_rows, :] = (sums[group][0] * SCALE).astype(BF16)
            grad_t[value_rows, :] = sums[group][1].astype(BF16)
            if group in hooks:
                hooks[group]()

    stagger((soften, combine, project))
    for n in range(3):
        cols = slice(n * 256, n * 256 + 256)
        grad[:, cols] = grad_t[cols, :].T
    for n in range(4):
        cols = slice(n * 256, n * 256 + 256)
        normed_grad[:, cols] = nt(grad[...], qkv[cols, :])
    for step in range(SEQ // ROWS):
        rows = slice(step * ROWS, step * ROWS + ROWS)
        inv = inverse[rows, :][:, :1]
        scaled = x(rows) * inv
        hat = normed_grad[rows, :]
        both = hat * scaled
        partial = both[:8]
        for k in range(1, ROWS // 8):
            partial = partial + both[k * 8 : k * 8 + 8]
        gain_sum[...] += partial
        mean = jnp.mean(both * gain[...], axis=1, keepdims=True)
        moved = inv * (hat * gain[...] - scaled * mean)
        result[rows, :] = (upstream[rows, :].astype(F32) + moved).astype(BF16)


def out_terms(q, att_t, upstream, piece):
    heads = pl.ds(pl.multiple_of(q * 128, 128), 128)
    for n in range(4):
        wide = slice(n * 256, n * 256 + 256)
        part = nn(att_t[0][heads, :], upstream[0][:, wide]) + nn(att_t[1][heads, :], upstream[1][:, wide])
        for core in range(2):
            for k in range(2):
                at = (2 * n + k) * HD
                block = part[core * HD : core * HD + HD, k * 128 : k * 128 + 128]
                piece[core, at : at + HD, :] = block.astype(BF16)


def qkv_terms(q, grad_t, normed, gain_sum, piece):
    cols = pl.ds(pl.multiple_of(q * 256, 256), 256)
    for m in range(3):
        rows = slice(m * 256, m * 256 + 256)
        part = nn(grad_t[0][rows, :], normed[0][:, cols]) + nn(grad_t[1][rows, :], normed[1][:, cols])
        for core in range(2):
            at = QW + m * 256
            piece[core, at : at + 256, :] = part[:, core * 128 : core * 128 + 128].astype(BF16)
    for core in range(2):
        lanes = pl.ds(pl.multiple_of(q * 256 + core * 128, 128), 128)
        row = jnp.sum(gain_sum[:, lanes], axis=0, keepdims=True)
        piece[core, QW + QKV :, :] = jnp.broadcast_to(row, (16, 128)).astype(BF16)


SCRATCH = {
    "orders": pltpu.SMEM((2, 1, 2), jnp.int32),
    "offsets": pltpu.SMEM((2, 1, 1, 2), jnp.int32),
    "number_sem": pltpu.SemaphoreType.DMA((2,)),
    "acts": pltpu.VMEM((2, 2, SEQ, D), BF16),
    "tops": pltpu.VMEM((2, SEQ, D), BF16),
    "seeds": pltpu.VMEM((2, SEQ, D), BF16),
    "gains": pltpu.VMEM((2, 1, D), F32),
    "qkvs": pltpu.VMEM((2, D, QKV), BF16),
    "outs": pltpu.VMEM((2, QW, D), BF16),
    "taken": pltpu.VMEM((2, SEQ, D), BF16),
    "normed": pltpu.VMEM((2, 2, SEQ, D), BF16),
    "grad_t": pltpu.VMEM((2, 2, QKV, SEQ), BF16),
    "att_t": pltpu.VMEM((2, 2, QW, SEQ), BF16),
    "gain_sum": pltpu.VMEM((2, 8, D), F32),
    "inverse": pltpu.VMEM((2, SEQ, 128), F32),
    "proj_t": pltpu.VMEM((2, QKV, SEQ), BF16),
    "keys": pltpu.VMEM((2, 2, SEQ, HD), BF16),
    "values": pltpu.VMEM((2, 2, SEQ, HD), BF16),
    "soft": pltpu.VMEM((2, HEADS, SEQ, SEQ), F32),
    "soft_low": pltpu.VMEM((2, HEADS, SEQ, SEQ), BF16),
    "ceiling": pltpu.VMEM((SEQ, SEQ), F32),
    "att_grad": pltpu.VMEM((QW, SEQ), BF16),
    "soft_grad": pltpu.VMEM((4, SEQ, SEQ), F32),
    "score_grad": pltpu.VMEM((HEADS, SEQ, SEQ), BF16),
    "grad": pltpu.VMEM((SEQ, QKV), BF16),
    "normed_grad": pltpu.VMEM((SEQ, D), F32),
    "pieces": pltpu.VMEM((2, 4, 2, PIECE, 128), BF16),
    "paired": pltpu.VMEM((2, 4, PIECE, 128), BF16),
    "own": pltpu.VMEM((2, 4, PIECE, 128), BF16),
    "mirror": pltpu.VMEM((4, PIECE, 128), BF16),
    "ring": pltpu.VMEM((2, 4, PIECE, 128), BF16),
    "load_sem": pltpu.SemaphoreType.DMA((6, 2)),
    "shift_sem": pltpu.SemaphoreType.DMA((2, 2)),
    "pair_sem": pltpu.SemaphoreType.DMA((2, 2, 2, 4)),
    "fold_sem": pltpu.SemaphoreType.DMA((2, 3, 4)),
    "ring_sem": pltpu.SemaphoreType.DMA((2, 2, 4, 4)),
}
VMEM_MB = 44
LOADS = ("acts", "tops", "gains", "qkvs", "outs", "seeds")
AHEAD = ((0, 0), (1, 3), (0, 3))
BEHIND = ((0, 1), (1, 1), (0, 2))


def window(*refs):
    sources = refs[2:14]
    grads, grad_gain, grad_qkv, grad_out = refs[14:18]
    s = dict(zip(SCRATCH, refs[18:]))
    orders, offsets = s["orders"], s["offsets"]
    numbers = [
        pltpu.make_async_copy(refs[k], into, s["number_sem"].at[k]) for k, into in enumerate((orders, offsets))
    ]
    for copy in numbers:
        copy.start()

    section, replica = lax.axis_index("section"), lax.axis_index("dp")
    sections, replicas = lax.axis_size("section"), lax.axis_size("dp")
    low, core = section % 2, replica % 2
    height = (replica // 2) * 2 + low
    partner = (section, replica + 1 - 2 * core)
    across = (sections - 2 - section + 2 * low, replica)
    ways = (
        (section + 1 - 2 * low, (replica + 2 * low) % replicas),
        (section + 1 - 2 * low, (replica + replicas - 2 + 2 * low) % replicas),
    )
    nexts = (((section + 1) % sections, replica), ((section + sections - 1) % sections, replica))

    barrier = pltpu.get_barrier_semaphore()
    for peer in (partner, across, *ways, *nexts):
        pl.semaphore_signal(barrier, inc=1, device_id=peer, device_id_type=MESH)

    def load(name, c):
        where = LOADS.index(name)
        return pltpu.make_async_copy(sources[2 * where + c], s[name].at[pl.ds(c, 1)], s["load_sem"].at[where, c])

    def picked(c, slot):
        chosen = orders[1 - c, 0, slot]
        offset = jnp.where(chosen == 0, offsets[1 - c, 0, 0, 0], offsets[1 - c, 0, 0, 1])

        def rows_of(rows):
            return jnp.where(chosen == 0, s["acts"][c, 0, rows, :].astype(F32), s["acts"][c, 1, rows, :].astype(F32))

        return rows_of, offset

    def keep(c, slot):
        names = ("proj_t", "keys", "values", "soft", "soft_low")
        return (*(s[name].at[c] for name in names), s["att_t"].at[c, slot])

    def run_norm(c, slot):
        norm_rows(picked(c, slot)[0], s["gains"].at[c], s["normed"].at[c, slot], s["inverse"].at[c])

    def run_forward(c, slot):
        set_ceiling(picked(c, slot)[1], s["ceiling"])
        forward(s["ceiling"], s["normed"].at[c, slot], s["qkvs"].at[c], keep(c, slot))

    def run_backward(c, slot, upstream, hooks=()):
        work = tuple(s[name] for name in ("att_grad", "soft_grad", "score_grad", "grad", "normed_grad"))
        backward(
            picked(c, slot)[0], s["gains"].at[c], s["inverse"].at[c], s["qkvs"].at[c], s["outs"].at[c],
            upstream, keep(c, slot), work, s["grad_t"].at[c, slot], s["gain_sum"].at[c],
            grads.at[1 - c, 0, slot], hooks,
        )

    def remote(source, target, sems, device):
        return pltpu.make_async_remote_copy(
            src_ref=source, dst_ref=target, send_sem=sems[0], recv_sem=sems[1],
            device_id=device, device_id_type=MESH,
        )

    def shift(c):
        sems = (s["shift_sem"].at[0, c], s["shift_sem"].at[1, c])
        return remote(grads.at[1 - c, 0, 0], s["taken"].at[c], sems, nexts[c])

    def pair(c, b, j):
        sems = (s["pair_sem"].at[0, c, b, j], s["pair_sem"].at[1, c, b, j])
        rows = BLOCKS[b]
        return remote(s["pieces"].at[c, j, 1 - core, rows], s["paired"].at[c, j, rows], sems, partner)

    def fold(f, j):
        sems = (s["fold_sem"].at[0, f, j], s["fold_sem"].at[1, f, j])
        rows = FOLDS[f]
        return remote(s["own"].at[0, j, rows], s["mirror"].at[j, rows], sems, across)

    def add_pair(c, b, j):
        rows = BLOCKS[b]
        pair(c, b, j).wait_recv()
        total = s["pieces"][c, j, core, rows, :].astype(F32) + s["paired"][c, j, rows, :].astype(F32)
        s["own"][c, j, rows, :] = total.astype(BF16)

    def chip(c, j):
        return ((height + 3 + c + 2 * j) % replicas) // 2

    def take(c):
        load("seeds", c).wait()
        shift(c).wait_recv()

        @pl.when(section == (sections - 1) * c)
        def _():
            s["taken"][c] = s["seeds"][c]

    def make_out_terms(c):
        for j in range(4):
            att_t = [s["att_t"].at[c, k] for k in range(2)]
            out_terms(chip(c, j), att_t, [s["tops"].at[c], s["taken"].at[c]], s["pieces"].at[c, j])
            pair(c, 0, j).start()

    def make_qkv_terms(c):
        for j in range(4):
            grad_t, normed = ([s[name].at[c, k] for k in range(2)] for name in ("grad_t", "normed"))
            qkv_terms(chip(c, j), grad_t, normed, s["gain_sum"].at[c], s["pieces"].at[c, j])
            pair(c, 1, j).start()

    def send_out_folds():
        for j in (0, 1, 3, 2):
            add_pair(0, 0, j)
            fold(0, j).start()

    def send_qkv_folds():
        for first, second in ((0, 1), (3, 2)):
            for j in (first, second):
                add_pair(0, 1, j)
            for j, f in ((first, 2), (second, 1), (first, 1), (second, 2)):
                fold(f, j).start()

    def term(way, step):
        if step == 0:
            return s["own"].at[1, 0]
        mirrored, j = (AHEAD, BEHIND)[way][step - 1]
        return s["mirror"].at[j] if mirrored == 0 else s["own"].at[1, j]

    def hop(way, step, p):
        sems = (s["ring_sem"].at[0, way, step, p], s["ring_sem"].at[1, way, step, p])
        return remote(term(way, step).at[PARTS[p]], s["ring"].at[way, step, PARTS[p]], sems, ways[way])

    folded = set()

    def send_on(way, step, p):
        rows = PARTS[p]
        if step > 0:
            mirrored, j = (AHEAD, BEHIND)[way][step - 1]
            if mirrored == 0 and (FOLD_OF[p], j) not in folded:
                folded.add((FOLD_OF[p], j))
                fold(FOLD_OF[p], j).wait_recv()
            if step > 1 or p % 2 == way:
                hop(way, step - 1, p).wait_recv()
                mine = term(way, step)
                total = mine[rows, :].astype(F32) + s["ring"][way, step - 1, rows, :].astype(F32)
                mine[rows, :] = total.astype(BF16)
        hop(way, step, p).start()

    def ring_step(b, step):
        if step == 0:
            for way in range(2):
                send_on(way, 0, 2 * b + way)
            return
        for turn in range(2):
            for way in range(2):
                send_on(way, step, 2 * b + (1 - way if turn == 0 else way))

    def final(b):
        for way in range(2):
            for p in (2 * b, 2 * b + 1):
                hop(way, 3, p).wait_recv()
        rows = BLOCKS[b]
        return s["own"][1, 2, rows].astype(F32) + s["ring"][0, 3, rows].astype(F32) + s["ring"][1, 3, rows].astype(F32)

    def ring_out_start():
        for j in (0, 3, 1, 2):
            add_pair(1, 0, j)
        ring_step(0, 0)

    for c in range(2):
        for name in ("acts", "gains", "qkvs", "outs", "tops"):
            load(name, c).start()
    for c in range(2):
        load("seeds", c).start()
    s["gain_sum"][...] = jnp.zeros_like(s["gain_sum"])

    for copy in numbers:
        copy.wait()
    for c in range(2):
        load("acts", c).wait()
        load("gains", c).wait()
        run_norm(c, 0)
        load("qkvs", c).wait()
        run_forward(c, 0)
        load("outs", c).wait()
        load("tops", c).wait()
        run_backward(c, 0, s["tops"].at[c])
        if c == 0:
            pl.semaphore_wait(barrier, 6)
        shift(c).start()
    for c in range(2):
        run_norm(c, 1)
        run_forward(c, 1)

    take(0)
    make_out_terms(0)
    run_backward(0, 1, s["taken"].at[0], {0: send_out_folds})
    make_qkv_terms(0)
    take(1)
    make_out_terms(1)
    run_backward(1, 1, s["taken"].at[1], {"start": send_qkv_folds, 0: ring_out_start})
    ring_step(0, 1)
    make_qkv_terms(1)
    ring_step(0, 2)
    for j in (0, 3, 1, 2):
        add_pair(1, 1, j)
    ring_step(1, 0)
    ring_step(0, 3)
    for step in range(1, 4):
        ring_step(1, step)

    total = final(0)
    for k in range(8):
        grad_out[0, :, k * 128 : k * 128 + 128] = total[k * HD : k * HD + HD, :]
    total = final(1)
    for n in range(3):
        grad_qkv[0, :, n * 256 : n * 256 + 256] = total[n * 256 : n * 256 + 256, :].T
    grad_gain[...] = total[QKV : QKV + 1, :]

    for c in range(2):
        shift(c).wait_send()
        for b in range(2):
            for j in range(4):
                pair(c, b, j).wait_send()
    for j in range(4):
        for f in range(3):
            fold(f, j).wait_send()
    for way in range(2):
        for step in range(4):
            for p in range(4):
                if step > 0 or p % 2 == way:
                    hop(way, step, p).wait_send()


def shards(
    act_down, act_up, grad_down, grad_up, seed_down, seed_up, gain_down, qkv_down, outproj_down,
    gain_up, qkv_up, outproj_up, doc_offsets, slot_order,
):
    shapes = (
        jax.ShapeDtypeStruct((2, 1, 2, SEQ, D), BF16),
        jax.ShapeDtypeStruct((1, 128), F32),
        jax.ShapeDtypeStruct((1, 128, QKV), F32),
        jax.ShapeDtypeStruct((1, HD, D), F32),
    )
    whole = pl.BlockSpec(memory_space=pltpu.VMEM)
    outside = pl.BlockSpec(memory_space=pltpu.HBM)
    return pl.pallas_call(
        window,
        in_specs=[outside] * 14,
        out_specs=[whole] * 4,
        out_shape=shapes,
        scratch_shapes=list(SCRATCH.values()),
        compiler_params=pltpu.CompilerParams(
            vmem_limit_bytes=VMEM_MB * 2**20, collective_id=0, has_side_effects=True
        ),
    )(
        *(
            pltpu.with_memory_space_constraint(x, pltpu.HBM)
            for x in (
                slot_order, doc_offsets.transpose(0, 1, 3, 2), act_up, act_down, grad_up, grad_down, gain_up[None], gain_down[None],
                qkv_up, qkv_down, outproj_up, outproj_down, seed_up[None], seed_down[None],
            )
        ),
    )


def solution(mesh):
    return jax.shard_map(
        shards,
        mesh=mesh,
        in_specs=(
            P("section", None, "dp", None),
            P("section", None, "dp", None),
            P("section", "dp", None),
            P("section", "dp", None),
            P("dp", None),
            P("dp", None),
            P("section", None),
            P("section", None, None),
            P("section", None, None),
            P("section", None),
            P("section", None, None),
            P("section", None, None),
            P(None, "section", None, "dp"),
            P(None, "section", None),
        ),
        out_specs=(
            P(None, "section", None, "dp", None),
            P("section", "dp"),
            P("section", "dp", None),
            P("section", "dp", None),
        ),
        check_vma=False,
    )
```

```python
import math

import jax
import jax.numpy as jnp
from jax import lax
from jax.experimental import pallas as pl
from jax.experimental.pallas import tpu as pltpu
from jax.sharding import PartitionSpec as P

F32, BF16 = jnp.float32, jnp.bfloat16
EPSILON = 1e-05
D, SEQ, HEADS, GROUP, HD = 1024, 256, 8, 4, 64
QW, QKV = 512, 768
ROWS = 32
PIECE = QKV + QW + 16
BLOCKS = (slice(0, QW), slice(QW, PIECE))
FOLDS = (slice(0, QW), slice(QW, 896), slice(896, PIECE))
PARTS = (slice(0, 256), slice(256, QW), slice(QW, 896), slice(896, PIECE))
FOLD_OF = (0, 0, 1, 2)
MESH = pl.DeviceIdType.MESH
SCALE = HD**-0.5
SCALE_2 = SCALE * math.log2(math.e)


def nn(a, b):
    return jnp.dot(a, b, preferred_element_type=F32)


def nt(a, b):
    return lax.dot_general(a, b, (((1,), (1,)), ((), ())), preferred_element_type=F32)


def stagger(stages):
    for step in range(HEADS + len(stages) - 1):
        for k, stage in enumerate(stages):
            if 0 <= step - k < HEADS:
                stage(step - k)


def norm_rows(x, gain, normed, inverse):
    for step in range(SEQ // ROWS):
        rows = slice(step * ROWS, step * ROWS + ROWS)
        xf = x(rows)
        inv = lax.rsqrt(jnp.mean(xf * xf, axis=1, keepdims=True) + EPSILON)
        normed[rows, :] = (xf * inv * gain[...]).astype(BF16)
        inverse[rows, :] = jnp.broadcast_to(inv, (ROWS, 128))


def set_ceiling(offset, ceiling):
    for half, depth in ((0, 128), (1, 256)):
        at_key = lax.broadcasted_iota(jnp.int32, (depth, 128), 0)
        at_query = lax.broadcasted_iota(jnp.int32, (depth, 128), 1) + half * 128
        allowed = (at_key <= at_query) & ((at_query < offset) | (at_key >= offset))
        ceiling[:depth, half * 128 : half * 128 + 128] = jnp.where(allowed, jnp.inf, -1e30)


def forward(ceiling, normed, qkv, keep, late=False):
    proj_t, keys, values, soft, soft_low, att_t = keep
    for n in range(3):
        cols = slice(n * 256, n * 256 + 256)
        part = nn(normed[...], qkv[:, cols])
        proj_t[cols, :] = part.T.astype(BF16)
        if n == 2:
            low = part.astype(BF16)
            keys[0], keys[1] = low[:, :64], low[:, 64:128]
            values[0], values[1] = low[:, 128:192], low[:, 192:256]
    def score(head):
        rows = slice(head * HD, head * HD + HD)
        soft[head] = nn(keys[head // GROUP], proj_t[rows, :])

    def normalize(head):
        for half, depth in ((0, 128), (1, 256)):
            cols = slice(half * 128, half * 128 + 128)
            part = jnp.minimum(soft[head, :depth, cols] * SCALE_2, ceiling[:depth, cols])
            raised = jnp.exp2(part - jnp.max(part, axis=0, keepdims=True))
            weights = raised * (1.0 / jnp.sum(raised, axis=0, keepdims=True))
            soft[head, :depth, cols] = weights
            soft_low[head, :depth, cols] = weights.astype(BF16)
        soft_low[head, 128:, :128] = jnp.zeros((128, 128), BF16)

    def attend(head):
        rows = slice(head * HD, head * HD + HD)
        value_rows = slice(QW + 128 + head // GROUP * HD, QW + 128 + head // GROUP * HD + HD)
        att_t[rows, :] = nn(proj_t[value_rows, :], soft_low[head]).astype(BF16)

    if late:
        stagger((score, normalize))
        return attend
    stagger((score, normalize, attend))


def backward(x, gain, inverse, qkv, outproj, upstream, keep, work, grad_t, gain_sum, result, hooks=()):
    hooks = dict(hooks)
    proj_t, keys, values, soft, soft_low, _ = keep
    att_grad, soft_grad, score_grad, grad, normed_grad = work
    for m in range(2):
        rows = slice(m * 256, m * 256 + 256)
        att_grad[rows, :] = nt(outproj[rows, :], upstream[...]).astype(BF16)
    if "start" in hooks:
        hooks["start"]()
    sums = [[None, None], [None, None]]

    def soften(head):
        rows = slice(head * HD, head * HD + HD)
        soft_grad[head % 4] = nn(values[head // GROUP], att_grad[rows, :])

    def combine(head):
        for half, depth in ((0, 128), (1, 256)):
            cols = slice(half * 128, half * 128 + 128)
            weights = soft[head, :depth, cols]
            part = soft_grad[head % 4, :depth, cols]
            total = jnp.sum(weights * part, axis=0, keepdims=True)
            score_grad[head, :depth, cols] = (weights * (part - total)).astype(BF16)
        score_grad[head, 128:, :128] = jnp.zeros((128, 128), BF16)

    def project(head):
        group = head // GROUP
        rows = slice(head * HD, head * HD + HD)
        key_rows = slice(QW + group * HD, QW + group * HD + HD)
        value_rows = slice(QW + 128 + group * HD, QW + 128 + group * HD + HD)
        grad_t[rows, :] = (nn(proj_t[key_rows, :], score_grad[head]) * SCALE).astype(BF16)
        for k, part in enumerate((nt(proj_t[rows, :], score_grad[head]), nt(att_grad[rows, :], soft_low[head]))):
            sums[group][k] = part if sums[group][k] is None else sums[group][k] + part
        if head % GROUP == GROUP - 1:
            grad_t[key_rows, :] = (sums[group][0] * SCALE).astype(BF16)
            grad_t[value_rows, :] = sums[group][1].astype(BF16)
            if group in hooks:
                hooks[group]()

    stagger((soften, combine, project))
    for n in range(3):
        cols = slice(n * 256, n * 256 + 256)
        grad[:, cols] = grad_t[cols, :].T
    for step in range(SEQ // ROWS):
        if step % 4 == 0:
            half = slice(step * ROWS, step * ROWS + 128)
            for n in range(4):
                cols = slice(n * 256, n * 256 + 256)
                normed_grad[half, cols] = nt(grad[half, :], qkv[cols, :])
            if step == 4 and "half" in hooks:
                hooks["half"]()
        rows = slice(step * ROWS, step * ROWS + ROWS)
        inv = inverse[rows, :][:, :1]
        scaled = x(rows) * inv
        hat = normed_grad[rows, :]
        both = hat * scaled
        partial = both[:8]
        for k in range(1, ROWS // 8):
            partial = partial + both[k * 8 : k * 8 + 8]
        gain_sum[...] += partial
        mean = jnp.mean(both * gain[...], axis=1, keepdims=True)
        moved = inv * (hat * gain[...] - scaled * mean)
        result[rows, :] = (upstream[rows, :].astype(F32) + moved).astype(BF16)


def out_terms(q, att_t, upstream, piece):
    heads = pl.ds(pl.multiple_of(q * 128, 128), 128)
    for n in range(4):
        wide = slice(n * 256, n * 256 + 256)
        part = nn(att_t[0][heads, :], upstream[0][:, wide]) + nn(att_t[1][heads, :], upstream[1][:, wide])
        for core in range(2):
            for k in range(2):
                at = (2 * n + k) * HD
                block = part[core * HD : core * HD + HD, k * 128 : k * 128 + 128]
                piece[core, at : at + HD, :] = block.astype(BF16)


def qkv_terms(q, grad_t, normed, gain_sum, piece):
    cols = pl.ds(pl.multiple_of(q * 256, 256), 256)
    for m in range(3):
        rows = slice(m * 256, m * 256 + 256)
        part = nn(grad_t[0][rows, :], normed[0][:, cols]) + nn(grad_t[1][rows, :], normed[1][:, cols])
        for core in range(2):
            at = QW + m * 256
            piece[core, at : at + 256, :] = part[:, core * 128 : core * 128 + 128].astype(BF16)
    for core in range(2):
        lanes = pl.ds(pl.multiple_of(q * 256 + core * 128, 128), 128)
        row = jnp.sum(gain_sum[:, lanes], axis=0, keepdims=True)
        piece[core, QW + QKV :, :] = jnp.broadcast_to(row, (16, 128)).astype(BF16)


SCRATCH = {
    "orders": pltpu.SMEM((2, 1, 2), jnp.int32),
    "offsets": pltpu.SMEM((2, 1, 1, 2), jnp.int32),
    "number_sem": pltpu.SemaphoreType.DMA((2,)),
    "acts": pltpu.VMEM((2, 2, SEQ, D), BF16),
    "tops": pltpu.VMEM((2, SEQ, D), BF16),
    "seeds": pltpu.VMEM((2, SEQ, D), BF16),
    "gains": pltpu.VMEM((2, 1, D), F32),
    "qkvs": pltpu.VMEM((2, D, QKV), BF16),
    "outs": pltpu.VMEM((2, QW, D), BF16),
    "taken": pltpu.VMEM((2, SEQ, D), BF16),
    "normed": pltpu.VMEM((2, 2, SEQ, D), BF16),
    "grad_t": pltpu.VMEM((2, 2, QKV, SEQ), BF16),
    "att_t": pltpu.VMEM((2, 2, QW, SEQ), BF16),
    "gain_sum": pltpu.VMEM((2, 8, D), F32),
    "inverse": pltpu.VMEM((2, SEQ, 128), F32),
    "proj_t": pltpu.VMEM((2, QKV, SEQ), BF16),
    "keys": pltpu.VMEM((2, 2, SEQ, HD), BF16),
    "values": pltpu.VMEM((2, 2, SEQ, HD), BF16),
    "soft": pltpu.VMEM((2, HEADS, SEQ, SEQ), F32),
    "soft_low": pltpu.VMEM((2, HEADS, SEQ, SEQ), BF16),
    "ceiling": pltpu.VMEM((SEQ, SEQ), F32),
    "att_grad": pltpu.VMEM((QW, SEQ), BF16),
    "soft_grad": pltpu.VMEM((4, SEQ, SEQ), F32),
    "score_grad": pltpu.VMEM((HEADS, SEQ, SEQ), BF16),
    "grad": pltpu.VMEM((SEQ, QKV), BF16),
    "normed_grad": pltpu.VMEM((SEQ, D), F32),
    "pieces": pltpu.VMEM((2, 4, 2, PIECE, 128), BF16),
    "paired": pltpu.VMEM((2, 4, PIECE, 128), BF16),
    "own": pltpu.VMEM((2, 4, PIECE, 128), BF16),
    "mirror": pltpu.VMEM((4, PIECE, 128), BF16),
    "ring": pltpu.VMEM((2, 4, PIECE, 128), BF16),
    "load_sem": pltpu.SemaphoreType.DMA((6, 2)),
    "shift_sem": pltpu.SemaphoreType.DMA((2, 2, 2)),
    "pair_sem": pltpu.SemaphoreType.DMA((2, 2, 2, 4)),
    "fold_sem": pltpu.SemaphoreType.DMA((2, 3, 4)),
    "ring_sem": pltpu.SemaphoreType.DMA((2, 2, 4, 4)),
}
VMEM_MB = 44
LOADS = ("acts", "tops", "gains", "qkvs", "outs", "seeds")
AHEAD = ((0, 0), (1, 3), (0, 3))
BEHIND = ((0, 1), (1, 1), (0, 2))


def window(*refs):
    sources = refs[2:14]
    grads, grad_gain, grad_qkv, grad_out = refs[14:18]
    s = dict(zip(SCRATCH, refs[18:]))
    orders, offsets = s["orders"], s["offsets"]
    numbers = [
        pltpu.make_async_copy(refs[k], into, s["number_sem"].at[k]) for k, into in enumerate((orders, offsets))
    ]
    for copy in numbers:
        copy.start()

    section, replica = lax.axis_index("section"), lax.axis_index("dp")
    sections, replicas = lax.axis_size("section"), lax.axis_size("dp")
    low, core = section % 2, replica % 2
    height = (replica // 2) * 2 + low
    partner = (section, replica + 1 - 2 * core)
    across = (sections - 2 - section + 2 * low, replica)
    ways = (
        (section + 1 - 2 * low, (replica + 2 * low) % replicas),
        (section + 1 - 2 * low, (replica + replicas - 2 + 2 * low) % replicas),
    )
    nexts = (((section + 1) % sections, replica), ((section + sections - 1) % sections, replica))

    barrier = pltpu.get_barrier_semaphore()
    for peer in (partner, across, *ways, *nexts):
        pl.semaphore_signal(barrier, inc=1, device_id=peer, device_id_type=MESH)

    def load(name, c):
        where = LOADS.index(name)
        return pltpu.make_async_copy(sources[2 * where + c], s[name].at[pl.ds(c, 1)], s["load_sem"].at[where, c])

    def picked(c, slot):
        chosen = orders[1 - c, 0, slot]
        offset = jnp.where(chosen == 0, offsets[1 - c, 0, 0, 0], offsets[1 - c, 0, 0, 1])

        def rows_of(rows):
            return jnp.where(chosen == 0, s["acts"][c, 0, rows, :].astype(F32), s["acts"][c, 1, rows, :].astype(F32))

        return rows_of, offset

    def keep(c, slot):
        names = ("proj_t", "keys", "values", "soft", "soft_low")
        return (*(s[name].at[c] for name in names), s["att_t"].at[c, slot])

    def run_norm(c, slot):
        norm_rows(picked(c, slot)[0], s["gains"].at[c], s["normed"].at[c, slot], s["inverse"].at[c])

    def run_forward(c, slot, late=False):
        set_ceiling(picked(c, slot)[1], s["ceiling"])
        return forward(s["ceiling"], s["normed"].at[c, slot], s["qkvs"].at[c], keep(c, slot), late)

    def run_backward(c, slot, upstream, hooks=()):
        work = tuple(s[name] for name in ("att_grad", "soft_grad", "score_grad", "grad", "normed_grad"))
        backward(
            picked(c, slot)[0], s["gains"].at[c], s["inverse"].at[c], s["qkvs"].at[c], s["outs"].at[c],
            upstream, keep(c, slot), work, s["grad_t"].at[c, slot], s["gain_sum"].at[c],
            grads.at[1 - c, 0, slot], hooks,
        )

    def remote(source, target, sems, device):
        return pltpu.make_async_remote_copy(
            src_ref=source, dst_ref=target, send_sem=sems[0], recv_sem=sems[1],
            device_id=device, device_id_type=MESH,
        )

    def shift(c, h):
        sems = (s["shift_sem"].at[0, c, h], s["shift_sem"].at[1, c, h])
        rows = pl.ds(h * 128, 128)
        return remote(grads.at[1 - c, 0, 0, rows], s["taken"].at[c, rows], sems, nexts[c])

    def pair(c, b, j):
        sems = (s["pair_sem"].at[0, c, b, j], s["pair_sem"].at[1, c, b, j])
        rows = BLOCKS[b]
        return remote(s["pieces"].at[c, j, 1 - core, rows], s["paired"].at[c, j, rows], sems, partner)

    def fold(f, j):
        sems = (s["fold_sem"].at[0, f, j], s["fold_sem"].at[1, f, j])
        rows = FOLDS[f]
        return remote(s["own"].at[0, j, rows], s["mirror"].at[j, rows], sems, across)

    def add_pair(c, b, j):
        rows = BLOCKS[b]
        pair(c, b, j).wait_recv()
        total = s["pieces"][c, j, core, rows, :].astype(F32) + s["paired"][c, j, rows, :].astype(F32)
        s["own"][c, j, rows, :] = total.astype(BF16)

    def chip(c, j):
        return ((height + 3 + c + 2 * j) % replicas) // 2

    def take(c):
        load("seeds", c).wait()
        for h in range(2):
            shift(c, h).wait_recv()

        @pl.when(section == (sections - 1) * c)
        def _():
            s["taken"][c] = s["seeds"][c]

    def make_out_terms(c):
        for j in range(4):
            att_t = [s["att_t"].at[c, k] for k in range(2)]
            out_terms(chip(c, j), att_t, [s["tops"].at[c], s["taken"].at[c]], s["pieces"].at[c, j])
            pair(c, 0, j).start()

    def make_qkv_terms(c):
        for j in range(4):
            grad_t, normed = ([s[name].at[c, k] for k in range(2)] for name in ("grad_t", "normed"))
            qkv_terms(chip(c, j), grad_t, normed, s["gain_sum"].at[c], s["pieces"].at[c, j])
            pair(c, 1, j).start()

    def send_out_folds():
        for j in (0, 1, 3, 2):
            add_pair(0, 0, j)
            fold(0, j).start()

    def send_qkv_folds():
        for first, second in ((0, 1), (3, 2)):
            for j in (first, second):
                add_pair(0, 1, j)
            for j, f in ((first, 2), (second, 1), (first, 1), (second, 2)):
                fold(f, j).start()

    def term(way, step):
        if step == 0:
            return s["own"].at[1, 0]
        mirrored, j = (AHEAD, BEHIND)[way][step - 1]
        return s["mirror"].at[j] if mirrored == 0 else s["own"].at[1, j]

    def hop(way, step, p):
        sems = (s["ring_sem"].at[0, way, step, p], s["ring_sem"].at[1, way, step, p])
        return remote(term(way, step).at[PARTS[p]], s["ring"].at[way, step, PARTS[p]], sems, ways[way])

    folded = set()

    def send_on(way, step, p):
        rows = PARTS[p]
        if step > 0:
            mirrored, j = (AHEAD, BEHIND)[way][step - 1]
            if mirrored == 0 and (FOLD_OF[p], j) not in folded:
                folded.add((FOLD_OF[p], j))
                fold(FOLD_OF[p], j).wait_recv()
            if step > 1 or p % 2 == way:
                hop(way, step - 1, p).wait_recv()
                mine = term(way, step)
                total = mine[rows, :].astype(F32) + s["ring"][way, step - 1, rows, :].astype(F32)
                mine[rows, :] = total.astype(BF16)
        hop(way, step, p).start()

    def ring_step(b, step):
        if step == 0:
            for way in range(2):
                send_on(way, 0, 2 * b + way)
            return
        for turn in range(2):
            for way in range(2):
                send_on(way, step, 2 * b + (1 - way if turn == 0 else way))

    def final(b):
        for way in range(2):
            for p in (2 * b, 2 * b + 1):
                hop(way, 3, p).wait_recv()
        rows = BLOCKS[b]
        return s["own"][1, 2, rows].astype(F32) + s["ring"][0, 3, rows].astype(F32) + s["ring"][1, 3, rows].astype(F32)

    def ring_out_start():
        add_pair(1, 0, 0)
        ring_step(0, 0)

    def start_both():
        ring_out_start()
        send_qkv_folds()

    def add_out_pairs():
        for j in (3, 1, 2):
            add_pair(1, 0, j)

    for c in range(2):
        for name in ("acts", "gains", "qkvs", "outs", "tops"):
            load(name, c).start()
    for c in range(2):
        load("seeds", c).start()
    s["gain_sum"][...] = jnp.zeros_like(s["gain_sum"])

    for copy in numbers:
        copy.wait()
    for c in range(2):
        load("acts", c).wait()
        load("gains", c).wait()
        run_norm(c, 0)
        load("qkvs", c).wait()
        attend = run_forward(c, 0, late=True)
        load("outs", c).wait()
        load("tops", c).wait()
        if c == 0:
            pl.semaphore_wait(barrier, 6)
            run_backward(c, 0, s["tops"].at[c], {"half": shift(c, 0).start})
            shift(c, 1).start()
        else:
            run_backward(c, 0, s["tops"].at[c])
        for head in range(HEADS):
            attend(head)
    for c in range(2):
        run_norm(c, 1)
        run_forward(c, 1)

    for h in range(2):
        shift(0, h).wait_send()
        shift(1, h).start()
    take(0)
    make_out_terms(0)
    run_backward(0, 1, s["taken"].at[0], {0: send_out_folds})
    make_qkv_terms(0)
    take(1)
    make_out_terms(1)
    run_backward(1, 1, s["taken"].at[1], {"start": start_both, 0: add_out_pairs})
    ring_step(0, 1)
    make_qkv_terms(1)
    ring_step(0, 2)
    add_pair(1, 1, 0)
    ring_step(1, 0)
    ring_step(0, 3)
    for j in (3, 1, 2):
        add_pair(1, 1, j)
    for step in range(1, 4):
        ring_step(1, step)

    total = final(0)
    for k in range(8):
        grad_out[0, :, k * 128 : k * 128 + 128] = total[k * HD : k * HD + HD, :]
    total = final(1)
    for n in range(3):
        grad_qkv[0, :, n * 256 : n * 256 + 256] = total[n * 256 : n * 256 + 256, :].T
    grad_gain[...] = total[QKV : QKV + 1, :]

    for c in range(2):
        if c == 1:
            for h in range(2):
                shift(c, h).wait_send()
        for b in range(2):
            for j in range(4):
                pair(c, b, j).wait_send()
    for j in range(4):
        for f in range(3):
            fold(f, j).wait_send()
    for way in range(2):
        for step in range(4):
            for p in range(4):
                if step > 0 or p % 2 == way:
                    hop(way, step, p).wait_send()


def shards(
    act_down, act_up, grad_down, grad_up, seed_down, seed_up, gain_down, qkv_down, outproj_down,
    gain_up, qkv_up, outproj_up, doc_offsets, slot_order,
):
    shapes = (
        jax.ShapeDtypeStruct((2, 1, 2, SEQ, D), BF16),
        jax.ShapeDtypeStruct((1, 128), F32),
        jax.ShapeDtypeStruct((1, 128, QKV), F32),
        jax.ShapeDtypeStruct((1, HD, D), F32),
    )
    whole = pl.BlockSpec(memory_space=pltpu.VMEM)
    outside = pl.BlockSpec(memory_space=pltpu.HBM)
    return pl.pallas_call(
        window,
        in_specs=[outside] * 14,
        out_specs=[whole] * 4,
        out_shape=shapes,
        scratch_shapes=list(SCRATCH.values()),
        compiler_params=pltpu.CompilerParams(
            vmem_limit_bytes=VMEM_MB * 2**20, collective_id=0, has_side_effects=True
        ),
    )(
        *(
            pltpu.with_memory_space_constraint(x, pltpu.HBM)
            for x in (
                slot_order, doc_offsets.transpose(0, 1, 3, 2), act_up, act_down, grad_up, grad_down, gain_up[None], gain_down[None],
                qkv_up, qkv_down, outproj_up, outproj_down, seed_up[None], seed_down[None],
            )
        ),
    )


def solution(mesh):
    return jax.shard_map(
        shards,
        mesh=mesh,
        in_specs=(
            P("section", None, "dp", None),
            P("section", None, "dp", None),
            P("section", "dp", None),
            P("section", "dp", None),
            P("dp", None),
            P("dp", None),
            P("section", None),
            P("section", None, None),
            P("section", None, None),
            P("section", None),
            P("section", None, None),
            P("section", None, None),
            P(None, "section", None, "dp"),
            P(None, "section", None),
        ),
        out_specs=(
            P(None, "section", None, "dp", None),
            P("section", "dp"),
            P("section", "dp", None),
            P("section", "dp", None),
        ),
        check_vma=False,
    )
```
